128 devices in a mesh: lon: 32 (over y, z, core), lat: 4 (over x).
Axes of the slice: x: 4, y: 4, z: 4, core: 2. Of those that a mesh axis runs over, the one named last changes fastest.
Arguments:
- spectrum: float32 [36, 36, 128, 512], P(None, None, 'lon', 'lat'), may hold values from 0.05 to 2
- sea_mask: int32 [128, 512], P('lon', 'lat'), may hold values 0 or 1
- refraction: float32 [2, 128, 512], P(None, 'lon', 'lat'), may hold values from -0.35 to 0.35
- atm_wind: float32 [2, 2, 16384], P(None, None, ('lon', 'lat')), may hold values from -20 to 20
- hour_fraction: float32 [1], replicated, may hold values from 0 to 1
- send_cells: int32 [128, 192], P(('lon', 'lat')), may hold values from 0 to 127, as said below
- recv_slots: int32 [4, 128, 512], P(None, 'lon', 'lat'), may hold values from 0 to 191, as said below
- recv_weights: float32 [4, 128, 512], P(None, 'lon', 'lat'), may hold values from 0.05 to 0.45
Outputs:
- spectrum_next: float32 [36, 36, 128, 512], P(None, None, 'lon', 'lat')
- surface_wind: float32 [2, 128, 512], P(None, 'lon', 'lat')
The draws below stay inside these ranges and needn't reach their ends.
Inputs may be any that keep to these rules, and one draw needn't show every extreme that they name: `send_cells`: row t holds, for each of the 32 wave tiles of tile t's latitude band in lon order, a block of 6 local atmosphere cells of tile t; every entry is read by some wave cell. `recv_slots`: entry e of a wave cell refers to position e % 6 of the block that the atmosphere tile at lon index e // 6 of the same latitude band lists for this cell's wave tile.
All inputs are finite; a program needn't handle non-finite values. No bound on the sum of `sea_mask` on one device may be relied on, other than what follows from the above.
Results may differ from the reference program's by a relative error of at most 0.0003.
Values sent between devices are 32-bit elements; how exact they have to be, the bound alone decides.
A program may use at most 128 MiB of HBM per device.

```python
import math
import jax
import jax.numpy as jnp
from jax import lax

FREQ = 36
DIRS = 36
CLON = 4
CLAT = 128
NSUB = 1
LON_TILES = 32
LAT_TILES = 4
TILES = 128
NLON = 128
NLAT = 512
ARW = 2
CAP = 6
ATM_DEV = 128
ATM = 16384


def slot_orders(key):
    order_key = jax.random.fold_in(key, 7)
    scores = jax.random.randint(order_key, (TILES, LON_TILES, CAP), 0, 1 << 20)
    scores = scores * CAP + jnp.arange(CAP, dtype=jnp.int32)
    ordering = jnp.argsort(scores, axis=-1, stable=True).astype(jnp.int32)
    inverse = jnp.argsort(ordering, axis=-1, stable=True).astype(jnp.int32)
    return (ordering, inverse)


def draw_send_cells(key, part):
    ordering, inverse = slot_orders(key)
    row_width = CLON // 2 + 1
    atm_row = ordering // row_width
    offset = ordering % row_width
    target = jnp.arange(LON_TILES, dtype=jnp.int32)[None, :, None]
    atm_lon = (target * (CLON // 2) + offset) % (NLON // 2)
    cells = atm_row * (NLON // 2) + atm_lon
    return cells.reshape(TILES, LON_TILES * CAP).astype(jnp.int32)


def draw_recv_slots(key, part):
    ordering, inverse = slot_orders(key)
    row_width = CLON // 2 + 1
    lon_cells = jnp.arange(NLON, dtype=jnp.int32)[:, None]
    lat_cells = jnp.arange(NLAT, dtype=jnp.int32)[None, :]
    lon_tile = lon_cells // CLON
    lon_local = lon_cells % CLON
    lat_tile = lat_cells // CLAT
    lat_local = lat_cells % CLAT
    slots_list = []
    for corner in range(4):
        offset = lon_local // 2 + corner % 2
        atm_row = jnp.minimum(lat_local // 2 + corner // 2, CLAT // 2 - 1)
        source_lon = atm_row // ARW
        canonical = atm_row % ARW * row_width + offset
        source_tile = source_lon * LAT_TILES + lat_tile
        slot_value = source_lon * CAP + inverse[source_tile, lon_tile, canonical]
        slots_list.append(slot_value)
    return jnp.stack(slots_list, axis=0).astype(jnp.int32)


def place_ends(values, stream_key, smallest, top_value):
    shape = values.shape
    index_at = [jax.random.randint(jax.random.fold_in(stream_key, axis), (), 0, shape[axis]) for axis in range(len(shape))]
    values = values.at[tuple(index_at)].set(smallest)
    longest = shape.index(max(shape))
    index_at[longest] = (index_at[longest] + 1) % shape[longest]
    return values.at[tuple(index_at)].set(top_value)


def steps_of(stream_key, shape, cuts, smallest, high):
    gain, own = 1.0, jax.random.fold_in(stream_key, 6)
    for axis_at, shards_of in cuts:
        steps = jnp.exp(jax.random.uniform(jax.random.fold_in(own, axis_at), (shards_of,), jnp.float32, smallest / len(cuts), high / len(cuts)))
        gain = gain * jnp.repeat(steps, shape[axis_at] // shards_of).reshape([-1 if axis == axis_at else 1 for axis in range(len(shape))])
    return gain


def setup_inputs(seed: int = 0) -> dict:
    keys = jax.random.split(jax.random.key(seed), 9)
    return {
        "spectrum": jnp.clip(jnp.exp(math.log(2.0) - 3.6888794 * jax.random.uniform(keys[0], (FREQ, DIRS, NLON, NLAT), jnp.float32) ** steps_of(keys[0], (FREQ, DIRS, NLON, NLAT), ((2, 32), (3, 4)), -0.2, 0.2)), 0.05, 2.0),
        "sea_mask": place_ends((jax.random.randint(keys[1], (NLON, NLAT), 0, 4) < 3).astype(jnp.int32), jax.random.fold_in(keys[1], 1), 0, 1),
        "refraction": jnp.clip(jax.random.uniform(keys[2], (2, NLON, NLAT), jnp.float32, -0.35, 0.35) * steps_of(keys[2], (2, NLON, NLAT), ((1, 32), (2, 4)), -0.4, 0.0), -0.35, 0.35),
        "atm_wind": jnp.clip(jax.random.uniform(keys[3], (2, 2, ATM), jnp.float32, -20.0, 20.0) * steps_of(keys[3], (2, 2, ATM), ((2, 128),), -0.4, 0.0), -20.0, 20.0),
        "hour_fraction": jnp.clip(jax.random.uniform(keys[4], (1,), jnp.float32, 0.0, 1.0), 0.0, 1.0),
        "send_cells": draw_send_cells(jax.random.fold_in(keys[8], 71), 0),
        "recv_slots": draw_recv_slots(jax.random.fold_in(keys[8], 71), 0),
        "recv_weights": jnp.clip(0.05 + 0.39999999 * jax.random.uniform(keys[7], (4, NLON, NLAT), jnp.float32) ** steps_of(keys[7], (4, NLON, NLAT), ((1, 32), (2, 4)), -0.2, 0.2), 0.05, 0.45),
    }


base_freq = 0.035
freq_step = 1.1
courant_max = 0.9
gravity = 9.81
input_rate = 0.05
damping_rate = 0.8
energy_ref = 0.5

def spectral_tables(freq_count, dir_count):
    frequencies = base_freq * freq_step ** jnp.arange(freq_count, dtype=jnp.float32)
    spacing = 2.0 * math.pi / dir_count
    angles = (jnp.arange(dir_count, dtype=jnp.float32) + 0.5) * spacing
    face_angles = (jnp.arange(dir_count, dtype=jnp.float32) + 1.0) * spacing
    return (frequencies, angles, face_angles)

def transport(padded, courant, dimension):
    length = padded.shape[dimension] - 4
    far_left = lax.slice_in_dim(padded, 0, length + 1, axis=dimension)
    left_cell = lax.slice_in_dim(padded, 1, length + 2, axis=dimension)
    right_cell = lax.slice_in_dim(padded, 2, length + 3, axis=dimension)
    far_right = lax.slice_in_dim(padded, 3, length + 4, axis=dimension)
    forward = courant > 0
    upwind = jnp.where(forward, left_cell, right_cell)
    downwind = jnp.where(forward, right_cell, left_cell)
    beyond = jnp.where(forward, far_left, far_right)
    magnitude = jnp.abs(courant)
    face_flux = courant * (upwind + 0.5 * (1.0 - magnitude) * (downwind - upwind) - (1.0 - magnitude * magnitude) / 6.0 * (downwind - 2.0 * upwind + beyond))
    return lax.slice_in_dim(face_flux, 1, length + 1, axis=dimension) - lax.slice_in_dim(face_flux, 0, length, axis=dimension)

def reference(spectrum, sea_mask, refraction, atm_wind, hour_fraction, send_cells, recv_slots, recv_weights):
    sea_frac = sea_mask.astype(jnp.float32)
    frequencies, angles, face_angles = spectral_tables(FREQ, DIRS)
    period_ratio = base_freq / frequencies
    courant_lon = courant_max * period_ratio[:, None] * jnp.cos(angles)[None, :]
    courant_lat = courant_max * period_ratio[:, None] * jnp.sin(angles)[None, :]
    bending = jnp.sqrt(period_ratio)
    face_sin = jnp.sin(face_angles)[:, None, None]
    face_cos = jnp.cos(face_angles)[:, None, None]

    def advance(inputs):
        density, along_lon, along_lat, bend_rate = inputs
        for substep in range(NSUB):
            padded = jnp.concatenate([density[:, -2:], density, density[:, :2]], axis=1)
            density = (density - transport(padded, along_lon[:, None, None], 1)) * sea_frac
            padded = jnp.pad(density, ((0, 0), (0, 0), (2, 2)))
            density = (density - transport(padded, along_lat[:, None, None], 2)) * sea_frac
        face_speed = bend_rate * (refraction[0][None] * face_sin - refraction[1][None] * face_cos)
        next_dir = jnp.roll(density, -1, axis=0)
        face_flux = jnp.maximum(face_speed, 0.0) * density + jnp.minimum(face_speed, 0.0) * next_dir
        return density - (face_flux - jnp.roll(face_flux, 1, axis=0))
    refracted = lax.map(advance, (spectrum, courant_lon, courant_lat, bending))
    weight_late = hour_fraction[0]
    wind_now = (1.0 - weight_late) * atm_wind[0] + weight_late * atm_wind[1]
    lon_cells = jnp.arange(NLON, dtype=jnp.int32)[:, None]
    lat_cells = jnp.arange(NLAT, dtype=jnp.int32)[None, :]
    lon_tile = (lon_cells // CLON).astype(jnp.int32)
    lat_tile = (lat_cells // CLAT).astype(jnp.int32)
    source_lon = (recv_slots // CAP).astype(jnp.int32)
    position = (recv_slots % CAP).astype(jnp.int32)
    source_tile = (source_lon * LAT_TILES + lat_tile[None]).astype(jnp.int32)
    local_cell = send_cells[source_tile, lon_tile[None] * CAP + position]
    picked = wind_now[:, (source_tile * ATM_DEV + local_cell).astype(jnp.int32)]
    surface_wind = lax.optimization_barrier(jnp.sum(recv_weights[None] * picked, axis=1))
    energy = lax.optimization_barrier(jnp.mean(refracted, axis=(0, 1)))
    energy_ratio = energy / energy_ref
    damping = energy_ratio * energy_ratio
    projected = surface_wind[0][None] * jnp.cos(angles)[:, None, None] + surface_wind[1][None] * jnp.sin(angles)[:, None, None]
    rel_freq = frequencies / frequencies[FREQ - 1]
    slowness_all = 2.0 * math.pi * frequencies / gravity

    def apply_sources(inputs):
        density, relative, slowness = inputs
        growth = input_rate * relative * jnp.maximum(projected * slowness - 1.0, 0.0)
        decay_rate = damping_rate * relative * damping
        return density * jnp.exp(growth - decay_rate)
    spectrum_next = lax.map(apply_sources, (refracted, rel_freq, slowness_all))
    return (spectrum_next, surface_wind)
```

```python
import functools
import math

import jax
import jax.numpy as jnp
import numpy as np
from jax import lax
from jax.experimental import pallas as pl
from jax.experimental.pallas import tpu as pltpu
from jax.sharding import PartitionSpec as P

FREQ = 36
DIRS = 36
QUAD = 9
LANES = 128
CELLS = 4
CAP = 6
BLOCKS = ((0, 8), (8, 8), (16, 8), (24, 8), (32, 4))
LOG2E = math.log2(math.e)
MESH = pl.DeviceIdType.MESH


def tables():
    k = np.arange(FREQ, dtype=np.float64)
    freq = 0.035 * 1.1**k
    ratio = 0.035 / freq
    rel = freq / freq[-1]
    slow = 2.0 * math.pi * freq / 9.81
    rows = np.stack(
        [0.9 * ratio, np.sqrt(ratio), LOG2E * 0.05 * rel * slow, LOG2E * 0.05 * rel]
    )
    per_freq = np.broadcast_to(rows[:, :, None], (4, FREQ, LANES)).astype(np.float32)
    decay = (LOG2E * 0.8 * rel * 4.0).astype(np.float32)
    theta = (np.arange(DIRS) + 0.5) * 2.0 * math.pi / DIRS
    phi = (np.arange(DIRS) + 1.0) * 2.0 * math.pi / DIRS
    per_dir = np.stack([np.cos(theta), np.sin(theta), np.sin(phi), np.cos(phi)], axis=1)
    return per_freq, per_dir.astype(np.float32), decay


def coefficients(rate, speed):
    a = rate * speed
    third = a * a * (1.0 / 6.0)
    g = a * (third - 1.0 / 6.0)
    b = a * ((third + 1.0 / 3.0) - 0.5 * a)
    p1 = (a - b) - (g + g)
    p0 = (1.0 - p1) - (g - b)
    return p0, p1, g, b


def take(table, index):
    return jnp.take_along_axis(table, index, axis=1, mode="promise_in_bounds")


def exchange_kernel(
    lon_size,
    lat_size,
    spec,
    sea_hbm,
    refr_hbm,
    atm_hbm,
    hour_hbm,
    cells_hbm,
    slots_hbm,
    weights_hbm,
    freq_hbm,
    dirs,
    out,
    energy_out,
    wind_out,
    xb,
    halo,
    packed,
    lat_in,
    merged,
    g_prev,
    e_sum,
    sea_i,
    refr,
    atm,
    hour,
    cells,
    slots,
    weights,
    freq,
    sea_b,
    r0_b,
    r1_b,
    u_b,
    v_b,
    wsend,
    wrecv,
    in_sem,
    x_sem,
    lon_send,
    lon_recv,
    lat_send,
    lat_recv,
    w_send,
    w_recv,
):
    me = lax.axis_index("lon")
    la = lax.axis_index("lat")
    right = lax.rem(me + 1, lon_size)
    left = lax.rem(me + lon_size - 1, lon_size)
    north = lax.rem(la + 1, lat_size)
    south = lax.rem(la + lat_size - 1, lat_size)

    barrier = pltpu.get_barrier_semaphore()

    def greet(d, carry):
        pl.semaphore_signal(
            barrier, inc=1, device_id=(lax.rem(me + d, lon_size), la), device_id_type=MESH
        )
        return carry

    lax.fori_loop(1, lon_size, greet, 0)
    for peer in (north, south):
        pl.semaphore_signal(barrier, inc=1, device_id=(me, peer), device_id_type=MESH)

    small = [
        (atm_hbm, atm),
        (hour_hbm, hour),
        (cells_hbm, cells),
        (sea_hbm, sea_i),
        (refr_hbm, refr),
        (slots_hbm, slots),
        (weights_hbm, weights),
        (freq_hbm, freq),
    ]
    small = [
        pltpu.make_async_copy(src, dst, in_sem.at[i]) for i, (src, dst) in enumerate(small)
    ]
    for copy in small:
        copy.start()

    def load(j, carry):
        for x in range(CELLS):
            pltpu.make_async_copy(spec.at[:, j, x, 0, :], xb.at[j, x], x_sem.at[j, x]).start()
        return carry

    lax.fori_loop(0, DIRS, load, 0)
    pl.semaphore_wait(barrier, lon_size + 1)

    def send_lon(j, x, slot, peer):
        pltpu.make_async_remote_copy(
            src_ref=spec.at[:, j, x, 0, :],
            dst_ref=halo.at[j, slot],
            send_sem=lon_send.at[j, slot],
            recv_sem=lon_recv.at[j, slot],
            device_id=(peer, la),
            device_id_type=MESH,
        ).start()

    def send_forward(j, carry):
        send_lon(j, 3, 0, right)
        send_lon(j, 0, 1, left)
        send_lon(j, 2, 2, right)
        return carry

    def send_backward(j, carry):
        send_lon(j, 3, 0, right)
        send_lon(j, 0, 1, left)
        send_lon(j, 1, 2, left)
        return carry

    lax.fori_loop(0, QUAD, send_forward, 0)
    lax.fori_loop(QUAD, 3 * QUAD, send_backward, 0)
    lax.fori_loop(3 * QUAD, DIRS, send_forward, 0)

    for copy in small:
        copy.wait()

    late = hour[0]
    wind = (1.0 - late) * atm[0] + late * atm[1]
    row = lax.broadcasted_iota(jnp.int32, (32, LANES), 0)
    lane32 = lax.broadcasted_iota(jnp.int32, (32, LANES), 1)
    six = lane32 - (lane32 // CAP) * CAP
    place = row * CAP + six
    tail = jnp.concatenate([cells[:, LANES:], jnp.zeros((1, 64), jnp.int32)], axis=1)
    head_b = jnp.broadcast_to(cells[:, :LANES], (32, LANES))
    tail_b = jnp.broadcast_to(tail, (32, LANES))
    low = take(head_b, jnp.minimum(place, LANES - 1))
    high = take(tail_b, jnp.maximum(place - LANES, 0))
    index = jnp.where(place < LANES, low, high)
    u_pick = take(jnp.broadcast_to(wind[0:1], (32, LANES)), index)
    v_pick = take(jnp.broadcast_to(wind[1:2], (32, LANES)), index)
    pick = jnp.where(lane32 < CAP, u_pick, v_pick)
    for i in range(32):
        wsend[i] = pick[i : i + 1]

    def send_wind(d, carry):
        peer = lax.rem(me + d, lon_size)
        pltpu.make_async_remote_copy(
            src_ref=wsend.at[peer],
            dst_ref=wrecv.at[me],
            send_sem=w_send.at[peer],
            recv_sem=w_recv.at[me],
            device_id=(peer, la),
            device_id_type=MESH,
        ).start()
        return carry

    lax.fori_loop(1, lon_size, send_wind, 0)
    wrecv[me] = wsend[me]

    sea = sea_i[...].astype(jnp.float32)
    r0 = refr[0]
    r1 = refr[1]
    for x in range(CELLS):
        sea_b[x] = jnp.broadcast_to(sea[x : x + 1], (8, LANES))
        r0_b[x] = jnp.broadcast_to(r0[x : x + 1], (8, LANES))
        r1_b[x] = jnp.broadcast_to(r1[x : x + 1], (8, LANES))
    e_sum[...] = jnp.zeros_like(e_sum)

    lane = lax.broadcasted_iota(jnp.int32, (8, LANES), 1)
    lane_three = lane - (lane // 3) * 3
    first = lane == 0
    last = lane == LANES - 1

    def lon_step(q):
        lon_forward = q in (0, 3)
        lat_forward = q < 2
        shift = 2 if lat_forward else 1
        packed[q] = jnp.zeros((FREQ, LANES), jnp.float32)

        def body(jl, carry):
            j = q * QUAD + jl
            for x in range(CELLS):
                pltpu.make_async_copy(spec.at[:, j, x, 0, :], xb.at[j, x], x_sem.at[j, x]).wait()
            for slot in range(3):
                pltpu.make_async_copy(
                    halo.at[j, slot], halo.at[j, slot], lon_recv.at[j, slot]
                ).wait()
            speed = dirs[j, 0] if lon_forward else -dirs[j, 0]
            base = jl * (3 * CELLS)
            for k0, n in BLOCKS:
                ks = pl.ds(k0, n)
                p0, p1, p2, pd = coefficients(freq[0, ks], speed)
                before = halo[j, 0, ks]
                after = halo[j, 1, ks]
                far = halo[j, 2, ks]
                own = [xb[j, x, ks] for x in range(CELLS)]
                if lon_forward:
                    line = [far, before] + own + [after]
                else:
                    line = [far, after] + own[::-1] + [before]
                pack = packed[q, ks]
                for i in range(CELLS):
                    x = i if lon_forward else CELLS - 1 - i
                    value = (p0 * line[i + 2] + p1 * line[i + 1]) + (
                        p2 * line[i] - pd * line[i + 3]
                    )
                    value = value * sea_b[x, :n]
                    xb[j, x, ks] = value
                    start = base + 3 * x
                    offset = lane[:n] - start
                    inside = (offset >= 0) & (offset < 3)
                    pack = jnp.where(inside, pltpu.roll(value, start + shift, 1), pack)
                packed[q, ks] = pack
            return carry

        lax.fori_loop(0, QUAD, body, 0)
        for side, peer in enumerate((north, south)):
            pltpu.make_async_remote_copy(
                src_ref=packed.at[q],
                dst_ref=lat_in.at[q, side],
                send_sem=lat_send.at[q, side],
                recv_sem=lat_recv.at[q, side],
                device_id=(me, peer),
                device_id_type=MESH,
            ).start()

    has_south = (la > 0).astype(jnp.float32)
    has_north = (la < lat_size - 1).astype(jnp.float32)

    def refract(jp, x, k0, n, here, ahead, behind):
        ks = pl.ds(k0, n)
        rate = r0_b[x, :n] * dirs[jp, 2] - r1_b[x, :n] * dirs[jp, 3]
        flux = (freq[1, ks] * rate) * jnp.where(rate > 0.0, here, ahead)
        return flux, (here - flux) + behind

    def growth(jp, x, k0, n):
        ks = pl.ds(k0, n)
        along = u_b[x, :n] * dirs[jp, 0] + v_b[x, :n] * dirs[jp, 1]
        return jnp.exp2(jnp.maximum(freq[2, ks] * along - freq[3, ks], 0.0))

    def put(j, x, k0, n, value):
        out[pl.ds(k0 * (DIRS * CELLS) + j * CELLS + x, n, stride=DIRS * CELLS), :] = value

    def lat_step(q):
        lat_forward = q < 2
        for side, peer in enumerate((north, south)):
            pltpu.make_async_copy(
                lat_in.at[q, side], lat_in.at[q, side], lat_recv.at[q, side]
            ).wait()
        for k0, n in BLOCKS:
            ks = pl.ds(k0, n)
            from_south = lat_in[q, 0, ks] * has_south
            from_north = lat_in[q, 1, ks] * has_north
            if lat_forward:
                value = jnp.where(lane_three[:n] == 2, from_north, from_south)
            else:
                value = jnp.where(lane_three[:n] == 0, from_south, from_north)
            merged[ks] = value

        def body(jl, carry):
            j = q * QUAD + jl
            jp = jnp.maximum(j - 1, 0)
            speed = dirs[j, 1] if lat_forward else -dirs[j, 1]
            base = jl * (3 * CELLS)
            for k0, n in BLOCKS:
                ks = pl.ds(k0, n)
                p0, p1, p2, pd = coefficients(freq[0, ks], speed)
                window = merged[ks]
                for x in range(CELLS):
                    start = base + 3 * x
                    f = xb[j, x, ks]
                    if lat_forward:
                        w = pltpu.roll(window, LANES + 126 - start, 1)
                        up2 = pltpu.roll(jnp.where(lane[:n] >= 126, w, f), 2, 1)
                        up1 = pltpu.roll(jnp.where(last[:n], w, f), 1, 1)
                        down = pltpu.roll(jnp.where(first[:n], w, f), 127, 1)
                    else:
                        w = pltpu.roll(window, LANES + 127 - start, 1)
                        up2 = pltpu.roll(jnp.where(lane[:n] < 2, w, f), 126, 1)
                        up1 = pltpu.roll(jnp.where(first[:n], w, f), 127, 1)
                        down = pltpu.roll(jnp.where(last[:n], w, f), 1, 1)
                    value = (p0 * f + p1 * up1) + (p2 * up2 - pd * down)
                    value = value * sea_b[x, :n]
                    xb[j, x, ks] = value
                    e_sum[x, ks] += value
                    flux, moved = refract(jp, x, k0, n, xb[jp, x, ks], value, g_prev[x, ks])
                    g_prev[x, ks] = flux
                    put(jp, x, k0, n, moved * growth(jp, x, k0, n))
            return carry

        lax.fori_loop(0, QUAD, body, 0)

    def finish_wind():
        def arrive(d, carry):
            peer = lax.rem(me + d, lon_size)
            pltpu.make_async_copy(wrecv.at[peer], wrecv.at[peer], w_recv.at[peer]).wait()
            return carry

        lax.fori_loop(1, lon_size, arrive, 0)
        table = jnp.concatenate([wrecv[i] for i in range(32)], axis=0)
        halves = []
        for part in range(2):
            spot = lane32 + part * LANES
            source = spot // CAP
            q = spot - source * CAP
            mine = source == row
            for comp in range(2):
                got = jnp.where(mine, take(table, q + comp * CAP), 0.0)
                halves.append(jnp.sum(got, axis=0, keepdims=True))
        slot = slots[...]
        low_slot = jnp.minimum(slot, LANES - 1)
        high_slot = jnp.maximum(slot - LANES, 0)
        winds = []
        for comp in range(2):
            low_b = jnp.broadcast_to(halves[comp], (16, LANES))
            high_b = jnp.broadcast_to(halves[2 + comp], (16, LANES))
            got = jnp.where(slot < LANES, take(low_b, low_slot), take(high_b, high_slot))
            got = got * weights[...]
            half = got[0:8] + got[8:16]
            winds.append(half[0:4] + half[4:8])
        wind_out[0] = winds[0]
        wind_out[1] = winds[1]
        for x in range(CELLS):
            u_b[x] = jnp.broadcast_to(winds[0][x : x + 1], (8, LANES))
            v_b[x] = jnp.broadcast_to(winds[1][x : x + 1], (8, LANES))

    lon_step(0)
    lon_step(1)
    finish_wind()
    lat_step(0)
    lon_step(2)
    lat_step(1)
    lon_step(3)
    lat_step(2)
    lat_step(3)

    for k0, n in BLOCKS:
        ks = pl.ds(k0, n)
        for x in range(CELLS):
            f0 = xb[0, x, ks]
            f_last = xb[DIRS - 1, x, ks]
            flux, moved = refract(DIRS - 1, x, k0, n, f_last, f0, g_prev[x, ks])
            put(DIRS - 1, x, k0, n, moved * growth(DIRS - 1, x, k0, n))
            _, moved = refract(0, x, k0, n, f0, xb[1, x, ks], flux)
            put(0, x, k0, n, moved * growth(0, x, k0, n))
    for x in range(CELLS):
        energy = jnp.sum(e_sum[x], axis=0, keepdims=True) * (1.0 / (FREQ * DIRS))
        energy_out[x : x + 1] = energy
        energy_out[x + 4 : x + 5] = energy

    def sent(j, carry):
        for slot in range(3):
            pltpu.make_async_copy(
                spec.at[:, j, 0, 0, :], halo.at[j, slot], lon_send.at[j, slot]
            ).wait()
        return carry

    lax.fori_loop(0, DIRS, sent, 0)
    for q in range(4):
        for side in range(2):
            pltpu.make_async_copy(packed.at[q], packed.at[q], lat_send.at[q, side]).wait()
    def wind_sent(d, carry):
        peer = lax.rem(me + d, lon_size)
        pltpu.make_async_copy(wsend.at[peer], wsend.at[peer], w_send.at[peer]).wait()
        return carry

    lax.fori_loop(1, lon_size, wind_sent, 0)


CHUNK = 4


def finish_kernel(moved, energy, wind, decay, out, wind_out, stage, wstage, sem, wsem):
    wstage[...] = wind[...]
    wcopy = pltpu.make_async_copy(wstage, wind_out, wsem)
    wcopy.start()
    e = energy[...]
    square = e * e

    def copy(c):
        ks = pl.ds(c * CHUNK, CHUNK)
        return pltpu.make_async_copy(stage.at[ks], out.at[ks], sem.at[c])

    def chunk(c, carry):
        for i in range(CHUNK):
            k = c * CHUNK + i
            factor = jnp.exp2(-(decay[k] * square))
            stage[k] = moved[k] * factor[None]
        copy(c).start()
        return carry

    lax.fori_loop(0, FREQ // CHUNK, chunk, 0)
    for c in range(FREQ // CHUNK):
        copy(c).wait()
    wcopy.wait()


def local(
    lon_size,
    lat_size,
    spectrum,
    sea_mask,
    refraction,
    atm_wind,
    hour_fraction,
    send_cells,
    recv_slots,
    recv_weights,
):
    per_freq, per_dir, decay = tables()
    f32 = jnp.float32
    hbm = pl.BlockSpec(memory_space=pltpu.HBM)
    vmem = pl.BlockSpec(memory_space=pltpu.VMEM)
    smem = pl.BlockSpec(memory_space=pltpu.SMEM)
    moved, energy, wind = pl.pallas_call(
        functools.partial(exchange_kernel, lon_size, lat_size),
        name="exchange",
        out_shape=(
            pltpu.VMEM((FREQ * DIRS * CELLS, LANES), f32),
            pltpu.VMEM((8, LANES), f32),
            pltpu.VMEM((2, CELLS, LANES), f32),
        ),
        in_specs=[hbm] * 9 + [smem],
        out_specs=(vmem, vmem, vmem),
        scratch_shapes=[
            pltpu.VMEM((DIRS, CELLS, FREQ, LANES), f32),
            pltpu.VMEM((DIRS, 3, FREQ, LANES), f32),
            pltpu.VMEM((4, FREQ, LANES), f32),
            pltpu.VMEM((4, 2, FREQ, LANES), f32),
            pltpu.VMEM((FREQ, LANES), f32),
            pltpu.VMEM((CELLS, FREQ, LANES), f32),
            pltpu.VMEM((CELLS, FREQ, LANES), f32),
            pltpu.VMEM((CELLS, LANES), jnp.int32),
            pltpu.VMEM((2, CELLS, LANES), f32),
            pltpu.VMEM((2, 2, LANES), f32),
            pltpu.SMEM((1,), f32),
            pltpu.VMEM((1, 192), jnp.int32),
            pltpu.VMEM((16, LANES), jnp.int32),
            pltpu.VMEM((16, LANES), f32),
            pltpu.VMEM((4, FREQ, LANES), f32),
            pltpu.VMEM((CELLS, 8, LANES), f32),
            pltpu.VMEM((CELLS, 8, LANES), f32),
            pltpu.VMEM((CELLS, 8, LANES), f32),
            pltpu.VMEM((CELLS, 8, LANES), f32),
            pltpu.VMEM((CELLS, 8, LANES), f32),
            pltpu.VMEM((32, 1, LANES), f32),
            pltpu.VMEM((32, 1, LANES), f32),
            pltpu.SemaphoreType.DMA((8,)),
            pltpu.SemaphoreType.DMA((DIRS, CELLS)),
            pltpu.SemaphoreType.DMA((DIRS, 3)),
            pltpu.SemaphoreType.DMA((DIRS, 3)),
            pltpu.SemaphoreType.DMA((4, 2)),
            pltpu.SemaphoreType.DMA((4, 2)),
            pltpu.SemaphoreType.DMA((32,)),
            pltpu.SemaphoreType.DMA((32,)),
        ],
        compiler_params=pltpu.CompilerParams(
            collective_id=0, has_side_effects=True, vmem_limit_bytes=54 << 20
        ),
    )(
        spectrum.reshape(FREQ, DIRS, CELLS, 1, LANES),
        sea_mask,
        refraction,
        atm_wind,
        hour_fraction,
        send_cells,
        recv_slots.reshape(4 * CELLS, LANES),
        recv_weights.reshape(4 * CELLS, LANES),
        jnp.asarray(per_freq),
        jnp.asarray(per_dir),
    )
    result, wind = pl.pallas_call(
        finish_kernel,
        name="finish",
        out_shape=(
            jax.ShapeDtypeStruct((FREQ, DIRS // 2, 8, LANES), f32),
            jax.ShapeDtypeStruct((2, CELLS, LANES), f32),
        ),
        in_specs=[vmem, vmem, vmem, smem],
        out_specs=(hbm, hbm),
        scratch_shapes=[
            pltpu.VMEM((FREQ, DIRS // 2, 8, LANES), f32),
            pltpu.VMEM((2, CELLS, LANES), f32),
            pltpu.SemaphoreType.DMA((FREQ // CHUNK,)),
            pltpu.SemaphoreType.DMA,
        ],
        compiler_params=pltpu.CompilerParams(vmem_limit_bytes=40 << 20),
    )(moved.reshape(FREQ, DIRS // 2, 8, LANES), energy, wind, jnp.asarray(decay))
    return result.reshape(FREQ, DIRS, CELLS, LANES), wind


def solution(mesh):
    in_specs = (
        P(None, None, "lon", "lat"),
        P("lon", "lat"),
        P(None, "lon", "lat"),
        P(None, None, ("lon", "lat")),
        P(),
        P(("lon", "lat"), None),
        P(None, "lon", "lat"),
        P(None, "lon", "lat"),
    )
    out_specs = (P(None, None, "lon", "lat"), P(None, "lon", "lat"))
    body = functools.partial(local, mesh.shape["lon"], mesh.shape["lat"])
    return jax.shard_map(body, mesh=mesh, in_specs=in_specs, out_specs=out_specs, check_vma=False)
```

```python
import functools
import math

import jax
import jax.numpy as jnp
import numpy as np
from jax import lax
from jax.experimental import pallas as pl
from jax.experimental.pallas import tpu as pltpu
from jax.sharding import PartitionSpec as P

FREQ = 36
DIRS = 36
QUAD = 9
SPAN = 3
GROUPS = 3
EDGE = 12
LANES = 128
CELLS = 4
CAP = 6
BLOCKS = ((0, 8), (8, 8), (16, 8), (24, 8), (32, 4))
LOG2E = math.log2(math.e)
MESH = pl.DeviceIdType.MESH


def tables():
    k = np.arange(FREQ, dtype=np.float64)
    freq = 0.035 * 1.1**k
    ratio = 0.035 / freq
    rel = freq / freq[-1]
    slow = 2.0 * math.pi * freq / 9.81
    rows = np.stack(
        [0.9 * ratio, np.sqrt(ratio), LOG2E * 0.05 * rel * slow, LOG2E * 0.05 * rel]
    )
    per_freq = np.broadcast_to(rows[:, :, None], (4, FREQ, LANES)).astype(np.float32)
    decay = (LOG2E * 0.8 * rel * 4.0).astype(np.float32)
    theta = (np.arange(DIRS) + 0.5) * 2.0 * math.pi / DIRS
    phi = (np.arange(DIRS) + 1.0) * 2.0 * math.pi / DIRS
    per_dir = np.stack([np.cos(theta), np.sin(theta), np.sin(phi), np.cos(phi)], axis=1)
    return per_freq, per_dir.reshape(-1).astype(np.float32), decay


def coefficients(rate, speed):
    a = rate * speed
    third = a * a * (1.0 / 6.0)
    g = a * (third - 1.0 / 6.0)
    b = a * ((third + 1.0 / 3.0) - 0.5 * a)
    p1 = (a - b) - (g + g)
    p0 = (1.0 - p1) - (g - b)
    return p0, p1, g, b


def take(table, index):
    return jnp.take_along_axis(table, index, axis=1, mode="promise_in_bounds")


def exchange_kernel(
    lon_size,
    lat_size,
    spec,
    spec_rows,
    sea_hbm,
    refr_hbm,
    atm_hbm,
    hour,
    cells_hbm,
    slots_hbm,
    weights_hbm,
    freq_hbm,
    dirs,
    out,
    energy_out,
    wind_out,
    nat,
    xb,
    halo,
    packed,
    lat_in,
    merged,
    g_prev,
    e_sum,
    sea_i,
    refr,
    atm,
    cells,
    slots,
    weights,
    freq,
    sea_b,
    r0_b,
    r1_b,
    u_b,
    v_b,
    wsend,
    wrecv,
    in_sem,
    x_sem,
    lon_send,
    lon_recv,
    lat_send,
    lat_recv,
    w_send,
    w_recv,
):
    me = lax.axis_index("lon")
    la = lax.axis_index("lat")
    right = lax.rem(me + 1, lon_size)
    left = lax.rem(me + lon_size - 1, lon_size)
    north = lax.rem(la + 1, lat_size)
    south = lax.rem(la + lat_size - 1, lat_size)

    barrier = pltpu.get_barrier_semaphore()

    def greet(d, carry):
        pl.semaphore_signal(
            barrier, inc=1, device_id=(lax.rem(me + d, lon_size), la), device_id_type=MESH
        )
        return carry

    lax.fori_loop(1, lon_size, greet, 0)
    for peer in (north, south):
        pl.semaphore_signal(barrier, inc=1, device_id=(me, peer), device_id_type=MESH)

    small = [
        (atm_hbm, atm),
        (cells_hbm, cells),
        (sea_hbm, sea_i),
        (refr_hbm, refr),
        (slots_hbm, slots),
        (weights_hbm, weights),
        (freq_hbm, freq),
    ]
    small = [
        pltpu.make_async_copy(src, dst, in_sem.at[i]) for i, (src, dst) in enumerate(small)
    ]
    for copy in small:
        copy.start()

    whole = pltpu.make_async_copy(spec_rows, nat, x_sem)
    whole.start()
    pl.semaphore_wait(barrier, lon_size + 1)

    def send_lon(j, x, slot, peer):
        pltpu.make_async_remote_copy(
            src_ref=spec.at[:, j, x, 0, :],
            dst_ref=halo.at[j // SPAN, (j % SPAN) * 3 + slot],
            send_sem=lon_send,
            recv_sem=lon_recv.at[j // SPAN],
            device_id=(peer, la),
            device_id_type=MESH,
        ).start()

    def send_forward(j, carry):
        send_lon(j, 3, 0, right)
        send_lon(j, 0, 1, left)
        send_lon(j, 2, 2, right)
        return carry

    def send_backward(j, carry):
        send_lon(j, 3, 0, right)
        send_lon(j, 0, 1, left)
        send_lon(j, 1, 2, left)
        return carry

    lax.fori_loop(0, QUAD, send_forward, 0)

    for copy in small:
        copy.wait()

    late = hour[0]
    wind = (1.0 - late) * atm[0] + late * atm[1]
    row = lax.broadcasted_iota(jnp.int32, (32, LANES), 0)
    lane32 = lax.broadcasted_iota(jnp.int32, (32, LANES), 1)
    six = lane32 - (lane32 // CAP) * CAP
    place = row * CAP + six
    tail = jnp.concatenate([cells[:, LANES:], jnp.zeros((1, 64), jnp.int32)], axis=1)
    head_b = jnp.broadcast_to(cells[:, :LANES], (32, LANES))
    tail_b = jnp.broadcast_to(tail, (32, LANES))
    low = take(head_b, jnp.minimum(place, LANES - 1))
    high = take(tail_b, jnp.maximum(place - LANES, 0))
    index = jnp.where(place < LANES, low, high)
    u_pick = take(jnp.broadcast_to(wind[0:1], (32, LANES)), index)
    v_pick = take(jnp.broadcast_to(wind[1:2], (32, LANES)), index)
    pick = jnp.where(lane32 < CAP, u_pick, v_pick)
    for i in range(32):
        wsend[i] = pick[i : i + 1]

    def send_wind(d, carry):
        peer = lax.rem(me + d, lon_size)
        pltpu.make_async_remote_copy(
            src_ref=wsend.at[peer],
            dst_ref=wrecv.at[me],
            send_sem=w_send,
            recv_sem=w_recv,
            device_id=(peer, la),
            device_id_type=MESH,
        ).start()
        return carry

    lax.fori_loop(1, lon_size, send_wind, 0)
    lax.fori_loop(QUAD, 3 * QUAD, send_backward, 0)
    lax.fori_loop(3 * QUAD, DIRS, send_forward, 0)
    wrecv[me] = wsend[me]

    sea = sea_i[...].astype(jnp.float32)
    r0 = refr[0]
    r1 = refr[1]
    for x in range(CELLS):
        sea_b[x] = jnp.broadcast_to(sea[x : x + 1], (8, LANES))
        r0_b[x] = jnp.broadcast_to(r0[x : x + 1], (8, LANES))
        r1_b[x] = jnp.broadcast_to(r1[x : x + 1], (8, LANES))
    e_sum[...] = jnp.zeros_like(e_sum)

    lane = lax.broadcasted_iota(jnp.int32, (8, LANES), 1)
    lane_three = lane - (lane // 3) * 3
    first = lane == 0
    last = lane == LANES - 1

    def rows_of(j, x, k0, n):
        return pl.ds(k0 * (DIRS * CELLS) + j * CELLS + x, n, stride=DIRS * CELLS)

    def lon_group(q, g):
        lon_forward = q in (0, 3)
        shift = 2 if q < 2 else 1
        group = q * GROUPS + g
        pltpu.make_async_copy(halo.at[group], halo.at[group], lon_recv.at[group]).wait()

        def body(jl, carry):
            j = group * SPAN + jl
            speed = dirs[4 * j] if lon_forward else -dirs[4 * j]
            for k0, n in BLOCKS:
                ks = pl.ds(k0, n)
                p0, p1, p2, pd = coefficients(freq[0, ks], speed)
                before = halo[group, 3 * jl, ks]
                after = halo[group, 3 * jl + 1, ks]
                far = halo[group, 3 * jl + 2, ks]
                own = [nat[rows_of(j, x, k0, n), :] for x in range(CELLS)]
                if lon_forward:
                    line = [far, before] + own + [after]
                else:
                    line = [far, after] + own[::-1] + [before]
                pack = pltpu.roll(packed[group, ks], EDGE, 1)
                for i in range(CELLS):
                    x = i if lon_forward else CELLS - 1 - i
                    value = (p0 * line[i + 2] + p1 * line[i + 1]) + (
                        p2 * line[i] - pd * line[i + 3]
                    )
                    value = value * sea_b[x, :n]
                    xb[j, x, ks] = value
                    inside = (lane[:n] >= 3 * x) & (lane[:n] < 3 * x + 3)
                    pack = jnp.where(inside, pltpu.roll(value, 3 * x + shift, 1), pack)
                packed[group, ks] = pack
            return carry

        lax.fori_loop(0, SPAN, body, 0)
        for side, peer in enumerate((north, south)):
            pltpu.make_async_remote_copy(
                src_ref=packed.at[group],
                dst_ref=lat_in.at[group, side],
                send_sem=lat_send.at[side],
                recv_sem=lat_recv.at[group],
                device_id=(me, peer),
                device_id_type=MESH,
            ).start()

    has_south = (la > 0).astype(jnp.float32)
    has_north = (la < lat_size - 1).astype(jnp.float32)

    def rows_at(jp):
        d = [dirs[4 * jp + i] for i in range(4)]
        rates = [r0_b[x] * d[2] - r1_b[x] * d[3] for x in range(CELLS)]
        signs = [rate > 0.0 for rate in rates]
        along = [u_b[x] * d[0] + v_b[x] * d[1] for x in range(CELLS)]
        return rates, signs, along

    def refract(rows, x, k0, n, here, ahead, behind):
        rates, signs, _ = rows
        flux = (freq[1, pl.ds(k0, n)] * rates[x][:n]) * jnp.where(signs[x][:n], here, ahead)
        return flux, (here - flux) + behind

    def growth(rows, x, k0, n):
        ks = pl.ds(k0, n)
        return jnp.exp2(jnp.maximum(freq[2, ks] * rows[2][x][:n] - freq[3, ks], 0.0))

    def put(j, x, k0, n, value):
        out[rows_of(j, x, k0, n), :] = value

    def lat_group(q, g):
        lat_forward = q < 2
        group = q * GROUPS + g
        pltpu.make_async_copy(lat_in.at[group], lat_in.at[group], lat_recv.at[group]).wait()
        for k0, n in BLOCKS:
            ks = pl.ds(k0, n)
            from_south = lat_in[group, 0, ks] * has_south
            from_north = lat_in[group, 1, ks] * has_north
            if lat_forward:
                value = jnp.where(lane_three[:n] == 2, from_north, from_south)
            else:
                value = jnp.where(lane_three[:n] == 0, from_south, from_north)
            merged[ks] = pltpu.roll(value, LANES - EDGE * (SPAN - 1), 1)

        def body(jl, carry):
            j = group * SPAN + jl
            jp = jnp.maximum(j - 1, 0)
            speed = dirs[4 * j + 1] if lat_forward else -dirs[4 * j + 1]
            rows = rows_at(jp)
            for k0, n in BLOCKS:
                ks = pl.ds(k0, n)
                p0, p1, p2, pd = coefficients(freq[0, ks], speed)
                window = merged[ks]
                merged[ks] = pltpu.roll(window, EDGE, 1)
                for x in range(CELLS):
                    f = xb[j, x, ks]
                    if lat_forward:
                        w = pltpu.roll(window, 126 - 3 * x, 1)
                        up2 = pltpu.roll(jnp.where(lane[:n] >= 126, w, f), 2, 1)
                        up1 = pltpu.roll(jnp.where(last[:n], w, f), 1, 1)
                        down = pltpu.roll(jnp.where(first[:n], w, f), 127, 1)
                    else:
                        w = pltpu.roll(window, 127 - 3 * x, 1)
                        up2 = pltpu.roll(jnp.where(lane[:n] < 2, w, f), 126, 1)
                        up1 = pltpu.roll(jnp.where(first[:n], w, f), 127, 1)
                        down = pltpu.roll(jnp.where(last[:n], w, f), 1, 1)
                    value = (p0 * f + p1 * up1) + (p2 * up2 - pd * down)
                    value = value * sea_b[x, :n]
                    xb[j, x, ks] = value
                    e_sum[x, ks] += value
                    flux, moved = refract(rows, x, k0, n, xb[jp, x, ks], value, g_prev[x, ks])
                    g_prev[x, ks] = flux
                    put(jp, x, k0, n, moved * growth(rows, x, k0, n))
            return carry

        lax.fori_loop(0, SPAN, body, 0)

    def finish_wind():
        pltpu.make_async_copy(wrecv.at[pl.ds(0, 31)], wrecv.at[pl.ds(0, 31)], w_recv).wait()
        table = jnp.concatenate([wrecv[i] for i in range(32)], axis=0)
        halves = []
        for part in range(2):
            spot = lane32 + part * LANES
            source = spot // CAP
            q = spot - source * CAP
            mine = source == row
            for comp in range(2):
                got = jnp.where(mine, take(table, q + comp * CAP), 0.0)
                halves.append(jnp.sum(got, axis=0, keepdims=True))
        slot = slots[...]
        low_slot = jnp.minimum(slot, LANES - 1)
        high_slot = jnp.maximum(slot - LANES, 0)
        winds = []
        for comp in range(2):
            low_b = jnp.broadcast_to(halves[comp], (16, LANES))
            high_b = jnp.broadcast_to(halves[2 + comp], (16, LANES))
            got = jnp.where(slot < LANES, take(low_b, low_slot), take(high_b, high_slot))
            got = got * weights[...]
            half = got[0:8] + got[8:16]
            winds.append(half[0:4] + half[4:8])
        wind_out[0] = winds[0]
        wind_out[1] = winds[1]
        for x in range(CELLS):
            u_b[x] = jnp.broadcast_to(winds[0][x : x + 1], (8, LANES))
            v_b[x] = jnp.broadcast_to(winds[1][x : x + 1], (8, LANES))

    def stage(q):
        def body(g, carry):
            if q < 4:
                lon_group(q, g)
            if q > 0:
                lat_group(q - 1, g)
            return carry

        lax.fori_loop(0, GROUPS, body, 0)

    whole.wait()
    stage(0)
    finish_wind()
    for q in range(1, 5):
        stage(q)

    rows_last = rows_at(DIRS - 1)
    rows_first = rows_at(0)
    for k0, n in BLOCKS:
        ks = pl.ds(k0, n)
        for x in range(CELLS):
            f0 = xb[0, x, ks]
            f_last = xb[DIRS - 1, x, ks]
            flux, moved = refract(rows_last, x, k0, n, f_last, f0, g_prev[x, ks])
            put(DIRS - 1, x, k0, n, moved * growth(rows_last, x, k0, n))
            _, moved = refract(rows_first, x, k0, n, f0, xb[1, x, ks], flux)
            put(0, x, k0, n, moved * growth(rows_first, x, k0, n))
    for x in range(CELLS):
        energy = jnp.sum(e_sum[x], axis=0, keepdims=True) * (1.0 / (FREQ * DIRS))
        energy_out[x : x + 1] = energy
        energy_out[x + 4 : x + 5] = energy

    pltpu.make_async_copy(halo, halo, lon_send).wait()
    for side in range(2):
        pltpu.make_async_copy(packed, packed, lat_send.at[side]).wait()
    pltpu.make_async_copy(wsend.at[pl.ds(0, 31)], wsend.at[pl.ds(0, 31)], w_send).wait()


CHUNK = 4


def finish_kernel(moved, energy, wind, decay, out, wind_out, stage, wstage, sem, wsem):
    wstage[...] = wind[...]
    wcopy = pltpu.make_async_copy(wstage, wind_out, wsem)
    wcopy.start()
    e = energy[...]
    square = e * e

    def copy(c):
        ks = pl.ds(c * CHUNK, CHUNK)
        return pltpu.make_async_copy(stage.at[ks], out.at[ks], sem.at[c])

    def chunk(c, carry):
        for i in range(CHUNK):
            k = c * CHUNK + i
            factor = jnp.exp2(-(decay[k] * square))
            stage[k] = moved[k] * factor[None]
        copy(c).start()
        return carry

    lax.fori_loop(0, FREQ // CHUNK, chunk, 0)
    for c in range(FREQ // CHUNK):
        copy(c).wait()
    wcopy.wait()


def local(
    lon_size,
    lat_size,
    spectrum,
    sea_mask,
    refraction,
    atm_wind,
    hour_fraction,
    send_cells,
    recv_slots,
    recv_weights,
):
    per_freq, per_dir, decay = tables()
    f32 = jnp.float32
    hbm = pl.BlockSpec(memory_space=pltpu.HBM)
    vmem = pl.BlockSpec(memory_space=pltpu.VMEM)
    smem = pl.BlockSpec(memory_space=pltpu.SMEM)
    moved, energy, wind = pl.pallas_call(
        functools.partial(exchange_kernel, lon_size, lat_size),
        name="exchange",
        out_shape=(
            pltpu.VMEM((FREQ * DIRS * CELLS, LANES), f32),
            pltpu.VMEM((8, LANES), f32),
            pltpu.VMEM((2, CELLS, LANES), f32),
        ),
        in_specs=[hbm] * 5 + [smem] + [hbm] * 4 + [smem],
        out_specs=(vmem, vmem, vmem),
        scratch_shapes=[
            pltpu.VMEM((FREQ * DIRS * CELLS, LANES), f32),
            pltpu.VMEM((DIRS, CELLS, FREQ, LANES), f32),
            pltpu.VMEM((4 * GROUPS, 3 * SPAN, FREQ, LANES), f32),
            pltpu.VMEM((4 * GROUPS, FREQ, LANES), f32),
            pltpu.VMEM((4 * GROUPS, 2, FREQ, LANES), f32),
            pltpu.VMEM((FREQ, LANES), f32),
            pltpu.VMEM((CELLS, FREQ, LANES), f32),
            pltpu.VMEM((CELLS, FREQ, LANES), f32),
            pltpu.VMEM((CELLS, LANES), jnp.int32),
            pltpu.VMEM((2, CELLS, LANES), f32),
            pltpu.VMEM((2, 2, LANES), f32),
            pltpu.VMEM((1, 192), jnp.int32),
            pltpu.VMEM((16, LANES), jnp.int32),
            pltpu.VMEM((16, LANES), f32),
            pltpu.VMEM((4, FREQ, LANES), f32),
            pltpu.VMEM((CELLS, 8, LANES), f32),
            pltpu.VMEM((CELLS, 8, LANES), f32),
            pltpu.VMEM((CELLS, 8, LANES), f32),
            pltpu.VMEM((CELLS, 8, LANES), f32),
            pltpu.VMEM((CELLS, 8, LANES), f32),
            pltpu.VMEM((32, 1, LANES), f32),
            pltpu.VMEM((32, 1, LANES), f32),
            pltpu.SemaphoreType.DMA((7,)),
            pltpu.SemaphoreType.DMA,
            pltpu.SemaphoreType.DMA,
            pltpu.SemaphoreType.DMA((4 * GROUPS,)),
            pltpu.SemaphoreType.DMA((2,)),
            pltpu.SemaphoreType.DMA((4 * GROUPS,)),
            pltpu.SemaphoreType.DMA,
            pltpu.SemaphoreType.DMA,
        ],
        compiler_params=pltpu.CompilerParams(
            collective_id=0, has_side_effects=True, vmem_limit_bytes=54 << 20
        ),
    )(
        spectrum.reshape(FREQ, DIRS, CELLS, 1, LANES),
        spectrum.reshape(FREQ * DIRS * CELLS, LANES),
        sea_mask,
        refraction,
        atm_wind,
        hour_fraction,
        send_cells,
        recv_slots.reshape(4 * CELLS, LANES),
        recv_weights.reshape(4 * CELLS, LANES),
        jnp.asarray(per_freq),
        jnp.asarray(per_dir),
    )
    result, wind = pl.pallas_call(
        finish_kernel,
        name="finish",
        out_shape=(
            jax.ShapeDtypeStruct((FREQ, DIRS // 2, 8, LANES), f32),
            jax.ShapeDtypeStruct((2, CELLS, LANES), f32),
        ),
        in_specs=[vmem, vmem, vmem, smem],
        out_specs=(hbm, hbm),
        scratch_shapes=[
            pltpu.VMEM((FREQ, DIRS // 2, 8, LANES), f32),
            pltpu.VMEM((2, CELLS, LANES), f32),
            pltpu.SemaphoreType.DMA((FREQ // CHUNK,)),
            pltpu.SemaphoreType.DMA,
        ],
        compiler_params=pltpu.CompilerParams(vmem_limit_bytes=40 << 20),
    )(moved.reshape(FREQ, DIRS // 2, 8, LANES), energy, wind, jnp.asarray(decay))
    return result.reshape(FREQ, DIRS, CELLS, LANES), wind


def solution(mesh):
    in_specs = (
        P(None, None, "lon", "lat"),
        P("lon", "lat"),
        P(None, "lon", "lat"),
        P(None, None, ("lon", "lat")),
        P(),
        P(("lon", "lat"), None),
        P(None, "lon", "lat"),
        P(None, "lon", "lat"),
    )
    out_specs = (P(None, None, "lon", "lat"), P(None, "lon", "lat"))
    body = functools.partial(local, mesh.shape["lon"], mesh.shape["lat"])
    return jax.shard_map(body, mesh=mesh, in_specs=in_specs, out_specs=out_specs, check_vma=False)
```

```python
import functools
import math

import jax
import jax.numpy as jnp
import numpy as np
from jax import lax
from jax.experimental import pallas as pl
from jax.experimental.pallas import tpu as pltpu
from jax.sharding import PartitionSpec as P

FREQ = 36
DIRS = 36
QUAD = 9
SPAN = 3
GROUPS = 3
SIDE = 4
EDGE = SIDE * 4
LANES = 128
CELLS = 4
CAP = 6
BLOCKS = ((0, 8), (8, 8), (16, 8), (24, 8), (32, 4))
LOG2E = math.log2(math.e)
MESH = pl.DeviceIdType.MESH


def tables():
    k = np.arange(FREQ, dtype=np.float64)
    freq = 0.035 * 1.1**k
    ratio = 0.035 / freq
    rel = freq / freq[-1]
    slow = 2.0 * math.pi * freq / 9.81
    rows = np.stack(
        [0.9 * ratio, np.sqrt(ratio), LOG2E * 0.05 * rel * slow, LOG2E * 0.05 * rel]
    )
    per_freq = np.broadcast_to(rows[:, :, None], (4, FREQ, LANES)).astype(np.float32)
    decay = (LOG2E * 0.8 * rel * 4.0).astype(np.float32)
    theta = (np.arange(DIRS) + 0.5) * 2.0 * math.pi / DIRS
    phi = (np.arange(DIRS) + 1.0) * 2.0 * math.pi / DIRS
    per_dir = np.stack([np.cos(theta), np.sin(theta), np.sin(phi), np.cos(phi)], axis=1)
    return per_freq, per_dir.reshape(-1).astype(np.float32), decay


def coefficients(rate, speed):
    a = rate * speed
    third = a * a * (1.0 / 6.0)
    g = a * (third - 1.0 / 6.0)
    b = a * ((third + 1.0 / 3.0) - 0.5 * a)
    p1 = (a - b) - (g + g)
    p0 = (1.0 - p1) - (g - b)
    return p0, p1, g, b


def take(table, index):
    return jnp.take_along_axis(table, index, axis=1, mode="promise_in_bounds")


def exchange_kernel(
    lon_size,
    lat_size,
    spec,
    spec_rows,
    sea_hbm,
    refr_hbm,
    atm_hbm,
    hour,
    cells_hbm,
    slots_hbm,
    weights_hbm,
    freq_hbm,
    dirs,
    out,
    energy_out,
    wind_out,
    nat,
    along_lon,
    field,
    f_prev,
    halo,
    packed,
    lat_in,
    merged,
    g_prev,
    e_sum,
    sea_i,
    refr,
    atm,
    cells,
    slots,
    weights,
    freq,
    sea_b,
    r0_b,
    r1_b,
    u_b,
    v_b,
    wsend,
    wrecv,
    in_sem,
    x_sem,
    lon_send,
    lon_recv,
    lat_send,
    lat_recv,
    w_send,
    w_recv,
):
    me = lax.axis_index("lon")
    la = lax.axis_index("lat")
    right = lax.rem(me + 1, lon_size)
    left = lax.rem(me + lon_size - 1, lon_size)
    north = lax.rem(la + 1, lat_size)
    south = lax.rem(la + lat_size - 1, lat_size)

    barrier = pltpu.get_barrier_semaphore()

    def greet(d, carry):
        pl.semaphore_signal(
            barrier, inc=1, device_id=(lax.rem(me + d, lon_size), la), device_id_type=MESH
        )
        return carry

    lax.fori_loop(1, lon_size, greet, 0)
    for peer in (north, south):
        pl.semaphore_signal(barrier, inc=1, device_id=(me, peer), device_id_type=MESH)

    small = [
        (atm_hbm, atm),
        (cells_hbm, cells),
        (sea_hbm, sea_i),
        (refr_hbm, refr),
        (slots_hbm, slots),
        (weights_hbm, weights),
        (freq_hbm, freq),
    ]
    small = [
        pltpu.make_async_copy(src, dst, in_sem.at[i]) for i, (src, dst) in enumerate(small)
    ]
    for copy in small:
        copy.start()

    whole = pltpu.make_async_copy(spec_rows, nat, x_sem)
    whole.start()
    pl.semaphore_wait(barrier, lon_size + 1)

    def send_lon(j, x, slot, peer):
        pltpu.make_async_remote_copy(
            src_ref=spec.at[:, j, x, 0, :],
            dst_ref=halo.at[j // SPAN, (j % SPAN) * 3 + slot],
            send_sem=lon_send,
            recv_sem=lon_recv.at[j // SPAN],
            device_id=(peer, la),
            device_id_type=MESH,
        ).start()

    def send_forward(j, carry):
        send_lon(j, 3, 0, right)
        send_lon(j, 0, 1, left)
        send_lon(j, 2, 2, right)
        return carry

    def send_backward(j, carry):
        send_lon(j, 3, 0, right)
        send_lon(j, 0, 1, left)
        send_lon(j, 1, 2, left)
        return carry

    lax.fori_loop(0, QUAD, send_forward, 0)

    for copy in small:
        copy.wait()

    late = hour[0]
    wind = (1.0 - late) * atm[0] + late * atm[1]
    row = lax.broadcasted_iota(jnp.int32, (32, LANES), 0)
    lane32 = lax.broadcasted_iota(jnp.int32, (32, LANES), 1)
    six = lane32 - (lane32 // CAP) * CAP
    place = row * CAP + six
    tail = jnp.concatenate([cells[:, LANES:], jnp.zeros((1, 64), jnp.int32)], axis=1)
    head_b = jnp.broadcast_to(cells[:, :LANES], (32, LANES))
    tail_b = jnp.broadcast_to(tail, (32, LANES))
    low = take(head_b, jnp.minimum(place, LANES - 1))
    high = take(tail_b, jnp.maximum(place - LANES, 0))
    index = jnp.where(place < LANES, low, high)
    u_pick = take(jnp.broadcast_to(wind[0:1], (32, LANES)), index)
    v_pick = take(jnp.broadcast_to(wind[1:2], (32, LANES)), index)
    pick = jnp.where(lane32 < CAP, u_pick, v_pick)
    for i in range(32):
        wsend[i] = pick[i : i + 1]

    def send_wind(d, carry):
        peer = lax.rem(me + d, lon_size)
        pltpu.make_async_remote_copy(
            src_ref=wsend.at[peer],
            dst_ref=wrecv.at[me],
            send_sem=w_send,
            recv_sem=w_recv,
            device_id=(peer, la),
            device_id_type=MESH,
        ).start()
        return carry

    lax.fori_loop(1, lon_size, send_wind, 0)
    lax.fori_loop(QUAD, 3 * QUAD, send_backward, 0)
    lax.fori_loop(3 * QUAD, DIRS, send_forward, 0)
    wrecv[me] = wsend[me]

    sea = sea_i[...].astype(jnp.float32)
    r0 = refr[0]
    r1 = refr[1]
    for x in range(CELLS):
        sea_b[x] = jnp.broadcast_to(sea[x : x + 1], (8, LANES))
        r0_b[x] = jnp.broadcast_to(r0[x : x + 1], (8, LANES))
        r1_b[x] = jnp.broadcast_to(r1[x : x + 1], (8, LANES))
    e_sum[...] = jnp.zeros_like(e_sum)

    lane = lax.broadcasted_iota(jnp.int32, (8, LANES), 1)
    spot_all = lane & (SIDE - 1)
    edge = (lane >= LANES - 2) | (lane < 2)

    def rows_of(j, x, k0, n):
        return pl.ds(k0 * (DIRS * CELLS) + j * CELLS + x, n, stride=DIRS * CELLS)

    def lon_wait(group):
        pltpu.make_async_copy(halo.at[group], halo.at[group], lon_recv.at[group]).wait()

    def lon_cells(lon_forward, group, jl):
        j = group * SPAN + jl
        speed = dirs[4 * j] if lon_forward else -dirs[4 * j]
        for k0, n in BLOCKS:
            ks = pl.ds(k0, n)
            p0, p1, p2, pd = coefficients(freq[0, ks], speed)
            before = halo[group, 3 * jl, ks]
            after = halo[group, 3 * jl + 1, ks]
            far = halo[group, 3 * jl + 2, ks]
            own = [nat[rows_of(j, x, k0, n), :] for x in range(CELLS)]
            if lon_forward:
                line = [far, before] + own + [after]
            else:
                line = [far, after] + own[::-1] + [before]
            pack = pltpu.roll(packed[group, ks], EDGE, 1)
            for i in range(CELLS):
                x = i if lon_forward else CELLS - 1 - i
                value = (p0 * line[i + 2] + p1 * line[i + 1]) + (
                    p2 * line[i] - pd * line[i + 3]
                )
                value = value * sea_b[x, :n]
                along_lon[j, x, ks] = value
                start = SIDE * x
                inside = (lane[:n] >= start) & (lane[:n] < start + SIDE)
                pack = jnp.where(inside, pltpu.roll(value, start + 2, 1), pack)
            packed[group, ks] = pack

    def lon_group(lon_forward, group):
        lon_wait(group)

        def body(jl, carry):
            lon_cells(lon_forward, group, jl)
            return carry

        lax.fori_loop(0, SPAN, body, 0)
        lat_send_edges(group)

    def lat_send_edges(group):
        for side, peer in enumerate((north, south)):
            pltpu.make_async_remote_copy(
                src_ref=packed.at[group],
                dst_ref=lat_in.at[group, side],
                send_sem=lat_send.at[side],
                recv_sem=lat_recv.at[group],
                device_id=(me, peer),
                device_id_type=MESH,
            ).start()

    has_south = (la > 0).astype(jnp.float32)
    has_north = (la < lat_size - 1).astype(jnp.float32)

    def rows_at(jp):
        d = [dirs[4 * jp + i] for i in range(4)]
        rates = [r0_b[x] * d[2] - r1_b[x] * d[3] for x in range(CELLS)]
        signs = [rate > 0.0 for rate in rates]
        along = [u_b[x] * d[0] + v_b[x] * d[1] for x in range(CELLS)]
        return rates, signs, along

    def refract(rows, x, k0, n, here, ahead, behind):
        rates, signs, _ = rows
        flux = (freq[1, pl.ds(k0, n)] * rates[x][:n]) * jnp.where(signs[x][:n], here, ahead)
        return flux, (here - flux) + behind

    def growth(rows, x, k0, n):
        ks = pl.ds(k0, n)
        return jnp.exp2(jnp.maximum(freq[2, ks] * rows[2][x][:n] - freq[3, ks], 0.0))

    def put(j, x, k0, n, value):
        out[rows_of(j, x, k0, n), :] = value

    def lat_prepare(lat_forward, group):
        pltpu.make_async_copy(lat_in.at[group], lat_in.at[group], lat_recv.at[group]).wait()
        j = group * SPAN
        sign = 1.0 if lat_forward else -1.0
        speeds = [sign * dirs[4 * (j + i) + 1] for i in range(SPAN)]
        speed = jnp.where(lane < EDGE, speeds[2], jnp.where(lane < 2 * EDGE, speeds[1], speeds[0]))
        for k0, n in BLOCKS:
            ks = pl.ds(k0, n)
            spot = spot_all[:n]
            from_south = lat_in[group, 0, ks] * has_south
            from_north = lat_in[group, 1, ks] * has_north
            _, p1, p2, pd = coefficients(freq[0, ks], speed[:n])
            value = jnp.where(spot < 2, from_south, from_north) - packed[group, ks]
            one = 1 if lat_forward else LANES - 1
            near, next_spot, down_spot = (2, 3, 1) if lat_forward else (1, 0, 2)
            up_one = pltpu.roll(value, one, 1)
            up_two = pltpu.roll(value, (2 * one) % LANES, 1)
            down = pltpu.roll(value, LANES - one, 1)
            value = p2 * jnp.where((spot == near) | (spot == next_spot), up_two, 0.0)
            value = value + p1 * jnp.where(spot == near, up_one, 0.0)
            value = value - pd * jnp.where(spot == down_spot, down, 0.0)
            merged[ks] = pltpu.roll(value, LANES - EDGE * (SPAN - 1), 1)

    def lat_cells(lat_forward, group, jl):
        j = group * SPAN + jl
        jp = jnp.maximum(j - 1, 0)
        speed = dirs[4 * j + 1] if lat_forward else -dirs[4 * j + 1]
        rows = rows_at(jp)
        two, one = (2, LANES - 1) if lat_forward else (LANES - 2, 1)
        for k0, n in BLOCKS:
            ks = pl.ds(k0, n)
            p0, p1, p2, pd = coefficients(freq[0, ks], speed)
            window = merged[ks]
            merged[ks] = pltpu.roll(window, EDGE, 1)
            for x in range(CELLS):
                f = along_lon[j, x, ks]
                extra = jnp.where(edge[:n], pltpu.roll(window, LANES - 2 - SIDE * x, 1), 0.0)
                shifted = pltpu.roll(f, two, 1)
                odd = pltpu.roll(p1 * shifted - pd * f, one, 1)
                value = (odd + extra) + (p0 * f + p2 * shifted)
                value = value * sea_b[x, :n]
                field[j, x, ks] = value
                e_sum[x, ks] += value
                flux, moved = refract(rows, x, k0, n, f_prev[x, ks], value, g_prev[x, ks])
                f_prev[x, ks] = value
                g_prev[x, ks] = flux
                put(jp, x, k0, n, moved * growth(rows, x, k0, n))

    def lat_group(lat_forward, group):
        lat_prepare(lat_forward, group)

        def body(jl, carry):
            lat_cells(lat_forward, group, jl)
            return carry

        lax.fori_loop(0, SPAN, body, 0)

    def finish_wind():
        pltpu.make_async_copy(wrecv.at[pl.ds(0, 31)], wrecv.at[pl.ds(0, 31)], w_recv).wait()
        table = jnp.concatenate([wrecv[i] for i in range(32)], axis=0)
        halves = []
        for part in range(2):
            spot = lane32 + part * LANES
            source = spot // CAP
            q = spot - source * CAP
            mine = source == row
            for comp in range(2):
                got = jnp.where(mine, take(table, q + comp * CAP), 0.0)
                halves.append(jnp.sum(got, axis=0, keepdims=True))
        slot = slots[...]
        low_slot = jnp.minimum(slot, LANES - 1)
        high_slot = jnp.maximum(slot - LANES, 0)
        winds = []
        for comp in range(2):
            low_b = jnp.broadcast_to(halves[comp], (16, LANES))
            high_b = jnp.broadcast_to(halves[2 + comp], (16, LANES))
            got = jnp.where(slot < LANES, take(low_b, low_slot), take(high_b, high_slot))
            got = got * weights[...]
            half = got[0:8] + got[8:16]
            winds.append(half[0:4] + half[4:8])
        wind_out[0] = winds[0]
        wind_out[1] = winds[1]
        for x in range(CELLS):
            u_b[x] = jnp.broadcast_to(winds[0][x : x + 1], (8, LANES))
            v_b[x] = jnp.broadcast_to(winds[1][x : x + 1], (8, LANES))

    whole.wait()

    def run(g, carry):
        turn = (g >= GROUPS) & (g < 3 * GROUPS)

        @pl.when((g < 4 * GROUPS) & jnp.logical_not(turn))
        def _():
            lon_group(True, g)

        @pl.when(turn)
        def _():
            lon_group(False, g)

        @pl.when(g == GROUPS)
        def _():
            finish_wind()

        @pl.when(turn)
        def _():
            lat_group(True, g - GROUPS)

        @pl.when(g >= 3 * GROUPS)
        def _():
            lat_group(False, g - GROUPS)

        return carry

    lax.fori_loop(0, 5 * GROUPS, run, 0)

    def close(x, carry):
        def row_of(jp):
            d = [dirs[4 * jp + i] for i in range(4)]
            return r0_b[x] * d[2] - r1_b[x] * d[3], u_b[x] * d[0] + v_b[x] * d[1]

        rate_last, along_last = row_of(DIRS - 1)
        rate_first, along_first = row_of(0)
        for k0, n in BLOCKS:
            ks = pl.ds(k0, n)
            f0 = field[0, x, ks]
            f_last = f_prev[x, ks]
            f1 = field[1, x, ks]
            bend = freq[1, ks]
            flux = (bend * rate_last[:n]) * jnp.where(rate_last[:n] > 0.0, f_last, f0)
            moved = (f_last - flux) + g_prev[x, ks]
            grow = jnp.exp2(jnp.maximum(freq[2, ks] * along_last[:n] - freq[3, ks], 0.0))
            put(DIRS - 1, x, k0, n, moved * grow)
            flux0 = (bend * rate_first[:n]) * jnp.where(rate_first[:n] > 0.0, f0, f1)
            moved = (f0 - flux0) + flux
            grow = jnp.exp2(jnp.maximum(freq[2, ks] * along_first[:n] - freq[3, ks], 0.0))
            put(0, x, k0, n, moved * grow)
        energy = jnp.sum(e_sum[x], axis=0, keepdims=True) * (1.0 / (FREQ * DIRS))
        energy_out[pl.ds(x, 1)] = energy
        energy_out[pl.ds(x + 4, 1)] = energy
        return carry

    lax.fori_loop(0, CELLS, close, 0)

    pltpu.make_async_copy(halo, halo, lon_send).wait()
    for side in range(2):
        pltpu.make_async_copy(packed, packed, lat_send.at[side]).wait()
    pltpu.make_async_copy(wsend.at[pl.ds(0, 31)], wsend.at[pl.ds(0, 31)], w_send).wait()


CHUNK = 4


def finish_kernel(moved, energy, wind, decay, out, wind_out, stage, wstage, sem, wsem):
    wstage[...] = wind[...]
    wcopy = pltpu.make_async_copy(wstage, wind_out, wsem)
    wcopy.start()
    e = energy[...]
    square = e * e

    def copy(c):
        ks = pl.ds(c * CHUNK, CHUNK)
        return pltpu.make_async_copy(stage.at[ks], out.at[ks], sem.at[c])

    def chunk(c, carry):
        for i in range(CHUNK):
            k = c * CHUNK + i
            factor = jnp.exp2(-(decay[k] * square))
            stage[k] = moved[k] * factor[None]
        copy(c).start()
        return carry

    lax.fori_loop(0, FREQ // CHUNK, chunk, 0)
    for c in range(FREQ // CHUNK):
        copy(c).wait()
    wcopy.wait()


def local(
    lon_size,
    lat_size,
    spectrum,
    sea_mask,
    refraction,
    atm_wind,
    hour_fraction,
    send_cells,
    recv_slots,
    recv_weights,
):
    per_freq, per_dir, decay = tables()
    f32 = jnp.float32
    hbm = pl.BlockSpec(memory_space=pltpu.HBM)
    vmem = pl.BlockSpec(memory_space=pltpu.VMEM)
    smem = pl.BlockSpec(memory_space=pltpu.SMEM)
    moved, energy, wind = pl.pallas_call(
        functools.partial(exchange_kernel, lon_size, lat_size),
        name="exchange",
        out_shape=(
            pltpu.VMEM((FREQ * DIRS * CELLS, LANES), f32),
            pltpu.VMEM((8, LANES), f32),
            pltpu.VMEM((2, CELLS, LANES), f32),
        ),
        in_specs=[hbm] * 5 + [smem] + [hbm] * 4 + [smem],
        out_specs=(vmem, vmem, vmem),
        scratch_shapes=[
            pltpu.VMEM((FREQ * DIRS * CELLS, LANES), f32),
            pltpu.VMEM((DIRS, CELLS, FREQ, LANES), f32),
            pltpu.VMEM((DIRS, CELLS, FREQ, LANES), f32),
            pltpu.VMEM((CELLS, FREQ, LANES), f32),
            pltpu.VMEM((4 * GROUPS, 3 * SPAN, FREQ, LANES), f32),
            pltpu.VMEM((4 * GROUPS, FREQ, LANES), f32),
            pltpu.VMEM((4 * GROUPS, 2, FREQ, LANES), f32),
            pltpu.VMEM((FREQ, LANES), f32),
            pltpu.VMEM((CELLS, FREQ, LANES), f32),
            pltpu.VMEM((CELLS, FREQ, LANES), f32),
            pltpu.VMEM((CELLS, LANES), jnp.int32),
            pltpu.VMEM((2, CELLS, LANES), f32),
            pltpu.VMEM((2, 2, LANES), f32),
            pltpu.VMEM((1, 192), jnp.int32),
            pltpu.VMEM((16, LANES), jnp.int32),
            pltpu.VMEM((16, LANES), f32),
            pltpu.VMEM((4, FREQ, LANES), f32),
            pltpu.VMEM((CELLS, 8, LANES), f32),
            pltpu.VMEM((CELLS, 8, LANES), f32),
            pltpu.VMEM((CELLS, 8, LANES), f32),
            pltpu.VMEM((CELLS, 8, LANES), f32),
            pltpu.VMEM((CELLS, 8, LANES), f32),
            pltpu.VMEM((32, 1, LANES), f32),
            pltpu.VMEM((32, 1, LANES), f32),
            pltpu.SemaphoreType.DMA((7,)),
            pltpu.SemaphoreType.DMA,
            pltpu.SemaphoreType.DMA,
            pltpu.SemaphoreType.DMA((4 * GROUPS,)),
            pltpu.SemaphoreType.DMA((2,)),
            pltpu.SemaphoreType.DMA((4 * GROUPS,)),
            pltpu.SemaphoreType.DMA,
            pltpu.SemaphoreType.DMA,
        ],
        compiler_params=pltpu.CompilerParams(
            collective_id=0, has_side_effects=True, vmem_limit_bytes=54 << 20
        ),
    )(
        spectrum.reshape(FREQ, DIRS, CELLS, 1, LANES),
        spectrum.reshape(FREQ * DIRS * CELLS, LANES),
        sea_mask,
        refraction,
        atm_wind,
        hour_fraction,
        send_cells,
        recv_slots.reshape(4 * CELLS, LANES),
        recv_weights.reshape(4 * CELLS, LANES),
        jnp.asarray(per_freq),
        jnp.asarray(per_dir),
    )
    result, wind = pl.pallas_call(
        finish_kernel,
        name="finish",
        out_shape=(
            jax.ShapeDtypeStruct((FREQ, DIRS // 2, 8, LANES), f32),
            jax.ShapeDtypeStruct((2, CELLS, LANES), f32),
        ),
        in_specs=[vmem, vmem, vmem, smem],
        out_specs=(hbm, hbm),
        scratch_shapes=[
            pltpu.VMEM((FREQ, DIRS // 2, 8, LANES), f32),
            pltpu.VMEM((2, CELLS, LANES), f32),
            pltpu.SemaphoreType.DMA((FREQ // CHUNK,)),
            pltpu.SemaphoreType.DMA,
        ],
        compiler_params=pltpu.CompilerParams(vmem_limit_bytes=40 << 20),
    )(moved.reshape(FREQ, DIRS // 2, 8, LANES), energy, wind, jnp.asarray(decay))
    return result.reshape(FREQ, DIRS, CELLS, LANES), wind


def solution(mesh):
    in_specs = (
        P(None, None, "lon", "lat"),
        P("lon", "lat"),
        P(None, "lon", "lat"),
        P(None, None, ("lon", "lat")),
        P(),
        P(("lon", "lat"), None),
        P(None, "lon", "lat"),
        P(None, "lon", "lat"),
    )
    out_specs = (P(None, None, "lon", "lat"), P(None, "lon", "lat"))
    body = functools.partial(local, mesh.shape["lon"], mesh.shape["lat"])
    return jax.shard_map(body, mesh=mesh, in_specs=in_specs, out_specs=out_specs, check_vma=False)
```

```python
import functools
import math

import jax
import jax.numpy as jnp
import numpy as np
from jax import lax
from jax.experimental import pallas as pl
from jax.experimental.pallas import tpu as pltpu
from jax.sharding import PartitionSpec as P

FREQ = 36
DIRS = 36
QUAD = 9
SPAN = 3
GROUPS = 3
SIDE = 4
EDGE = SIDE * 4
LANES = 128
CELLS = 4
CAP = 6
BLOCKS = ((0, 8), (8, 8), (16, 8), (24, 8), (32, 4))
FIRST = 2
DEPTH = 12
CLOSING = (DIRS - 2, DIRS - 1, 0)
LAG = 5
LOG2E = math.log2(math.e)
MESH = pl.DeviceIdType.MESH


def tables():
    k = np.arange(FREQ, dtype=np.float64)
    freq = 0.035 * 1.1**k
    ratio = 0.035 / freq
    rel = freq / freq[-1]
    slow = 2.0 * math.pi * freq / 9.81
    rows = np.stack(
        [0.9 * ratio, np.sqrt(ratio), LOG2E * 0.05 * rel * slow, LOG2E * 0.05 * rel]
    )
    per_freq = np.broadcast_to(rows[:, :, None], (4, FREQ, LANES)).astype(np.float32)
    decay = (LOG2E * 0.8 * rel * 4.0).astype(np.float32)
    theta = (np.arange(DIRS) + 0.5) * 2.0 * math.pi / DIRS
    phi = (np.arange(DIRS) + 1.0) * 2.0 * math.pi / DIRS
    per_dir = np.stack([np.cos(theta), np.sin(theta), np.sin(phi), np.cos(phi)], axis=1)
    return per_freq, per_dir.reshape(-1).astype(np.float32), decay


def coefficients(rate, speed):
    a = rate * speed
    third = a * a * (1.0 / 6.0)
    g = a * (third - 1.0 / 6.0)
    b = a * ((third + 1.0 / 3.0) - 0.5 * a)
    p1 = (a - b) - (g + g)
    p0 = (1.0 - p1) - (g - b)
    return p0, p1, g, b


def take(table, index):
    return jnp.take_along_axis(table, index, axis=1, mode="promise_in_bounds")


def exchange_kernel(
    lon_size,
    lat_size,
    spec,
    spec_rows,
    sea_hbm,
    refr_hbm,
    atm_hbm,
    hour,
    cells_hbm,
    slots_hbm,
    weights_hbm,
    freq_hbm,
    dirs,
    out,
    energy_out,
    wind_out,
    nat,
    along_lon,
    field,
    f_prev,
    coef,
    halo,
    packed,
    lat_in,
    merged,
    g_prev,
    e_sum,
    sea_i,
    refr,
    atm,
    cells,
    slots,
    weights,
    freq,
    sea_b,
    r0_b,
    r1_b,
    u_b,
    v_b,
    wsend,
    wrecv,
    in_sem,
    x_sem,
    lon_send,
    lon_recv,
    lat_send,
    lat_recv,
    w_send,
    w_recv,
):
    me = lax.axis_index("lon")
    la = lax.axis_index("lat")
    right = lax.rem(me + 1, lon_size)
    left = lax.rem(me + lon_size - 1, lon_size)
    north = lax.rem(la + 1, lat_size)
    south = lax.rem(la + lat_size - 1, lat_size)

    barrier = pltpu.get_barrier_semaphore()

    def greet(d, carry):
        pl.semaphore_signal(
            barrier, inc=1, device_id=(lax.rem(me + d, lon_size), la), device_id_type=MESH
        )
        return carry

    lax.fori_loop(1, lon_size, greet, 0)
    for peer in (north, south):
        pl.semaphore_signal(barrier, inc=1, device_id=(me, peer), device_id_type=MESH)

    small = [
        (atm_hbm, atm),
        (cells_hbm, cells),
        (sea_hbm, sea_i),
        (refr_hbm, refr),
        (slots_hbm, slots),
        (weights_hbm, weights),
        (freq_hbm, freq),
    ]
    small = [
        pltpu.make_async_copy(src, dst, in_sem.at[i]) for i, (src, dst) in enumerate(small)
    ]
    for copy in small:
        copy.start()

    whole = pltpu.make_async_copy(spec_rows, nat, x_sem)
    whole.start()
    pl.semaphore_wait(barrier, lon_size + 1)

    def send_lon(j, x, slot, peer):
        pltpu.make_async_remote_copy(
            src_ref=spec.at[:, j, x, 0, :],
            dst_ref=halo.at[j // SPAN, (j % SPAN) * 3 + slot],
            send_sem=lon_send,
            recv_sem=lon_recv.at[j // SPAN],
            device_id=(peer, la),
            device_id_type=MESH,
        ).start()

    def send_group(group, carry):
        turned = (group >= GROUPS) & (group < 3 * GROUPS)
        cell = jnp.where(turned, 1, 2)
        peer = jnp.where(turned, left, right)

        def one(jl, inner):
            j = group * SPAN + jl
            send_lon(j, 3, 0, right)
            send_lon(j, 0, 1, left)
            send_lon(j, cell, 2, peer)
            return inner

        lax.fori_loop(0, SPAN, one, 0)
        return carry

    lax.fori_loop(0, FIRST, send_group, 0)

    for copy in small:
        copy.wait()

    late = hour[0]
    wind = (1.0 - late) * atm[0] + late * atm[1]
    row = lax.broadcasted_iota(jnp.int32, (32, LANES), 0)
    lane32 = lax.broadcasted_iota(jnp.int32, (32, LANES), 1)
    six = lane32 - (lane32 // CAP) * CAP
    place = row * CAP + six
    tail = jnp.concatenate([cells[:, LANES:], jnp.zeros((1, 64), jnp.int32)], axis=1)
    head_b = jnp.broadcast_to(cells[:, :LANES], (32, LANES))
    tail_b = jnp.broadcast_to(tail, (32, LANES))
    low = take(head_b, jnp.minimum(place, LANES - 1))
    high = take(tail_b, jnp.maximum(place - LANES, 0))
    index = jnp.where(place < LANES, low, high)
    u_pick = take(jnp.broadcast_to(wind[0:1], (32, LANES)), index)
    v_pick = take(jnp.broadcast_to(wind[1:2], (32, LANES)), index)
    pick = jnp.where(lane32 < CAP, u_pick, v_pick)
    for i in range(32):
        wsend[i] = pick[i : i + 1]

    def send_wind(d, carry):
        peer = lax.rem(me + d, lon_size)
        pltpu.make_async_remote_copy(
            src_ref=wsend.at[peer],
            dst_ref=wrecv.at[me],
            send_sem=w_send,
            recv_sem=w_recv,
            device_id=(peer, la),
            device_id_type=MESH,
        ).start()
        return carry

    lax.fori_loop(1, lon_size, send_wind, 0)
    wrecv[me] = wsend[me]

    sea = sea_i[...].astype(jnp.float32)
    r0 = refr[0]
    r1 = refr[1]
    for x in range(CELLS):
        sea_b[x] = jnp.broadcast_to(sea[x : x + 1], (8, LANES))
        r0_b[x] = jnp.broadcast_to(r0[x : x + 1], (8, LANES))
        r1_b[x] = jnp.broadcast_to(r1[x : x + 1], (8, LANES))
    e_sum[...] = jnp.zeros_like(e_sum)

    lane = lax.broadcasted_iota(jnp.int32, (8, LANES), 1)
    spot_all = lane & (SIDE - 1)
    edge = (lane >= LANES - 2) | (lane < 2)

    def rows_of(j, x, k0, n):
        return pl.ds(k0 * (DIRS * CELLS) + j * CELLS + x, n, stride=DIRS * CELLS)

    def lon_wait(group):
        pltpu.make_async_copy(halo.at[group], halo.at[group], lon_recv.at[group]).wait()

    def lon_cells(lon_forward, group, jl):
        j = group * SPAN + jl
        for k0, n in BLOCKS:
            ks = pl.ds(k0, n)
            p0, p1, p2, pd = (coef[j, i, ks] for i in range(4))
            before = halo[group, 3 * jl, ks]
            after = halo[group, 3 * jl + 1, ks]
            far = halo[group, 3 * jl + 2, ks]
            own = [nat[rows_of(j, x, k0, n), :] for x in range(CELLS)]
            if lon_forward:
                line = [far, before] + own + [after]
            else:
                line = [far, after] + own[::-1] + [before]
            pack = pltpu.roll(packed[group, ks], EDGE, 1)
            for i in range(CELLS):
                x = i if lon_forward else CELLS - 1 - i
                value = (p0 * line[i + 2] + p1 * line[i + 1]) + (
                    p2 * line[i] - pd * line[i + 3]
                )
                value = value * sea_b[x, :n]
                along_lon[j, x, ks] = value
                start = SIDE * x
                inside = (lane[:n] >= start) & (lane[:n] < start + SIDE)
                pack = jnp.where(inside, pltpu.roll(value, start + 2, 1), pack)
            packed[group, ks] = pack

    def lon_group(lon_forward, group):
        lon_wait(group)

        def body(jl, carry):
            lon_cells(lon_forward, group, jl)
            return carry

        lax.fori_loop(0, SPAN, body, 0)
        lat_send_edges(group)

    def lat_send_edges(group):
        for side, peer in enumerate((north, south)):
            pltpu.make_async_remote_copy(
                src_ref=packed.at[group],
                dst_ref=lat_in.at[group, side],
                send_sem=lat_send.at[side],
                recv_sem=lat_recv.at[group],
                device_id=(me, peer),
                device_id_type=MESH,
            ).start()

    has_south = (la > 0).astype(jnp.float32)
    has_north = (la < lat_size - 1).astype(jnp.float32)

    def rows_at(jp):
        d = [dirs[4 * jp + i] for i in range(4)]
        rates = [r0_b[x] * d[2] - r1_b[x] * d[3] for x in range(CELLS)]
        signs = [rate > 0.0 for rate in rates]
        along = [u_b[x] * d[0] + v_b[x] * d[1] for x in range(CELLS)]
        return rates, signs, along

    def refract(rows, x, k0, n, here, ahead, behind):
        rates, signs, _ = rows
        flux = (freq[1, pl.ds(k0, n)] * rates[x][:n]) * jnp.where(signs[x][:n], here, ahead)
        return flux, (here - flux) + behind

    def growth(rows, x, k0, n):
        ks = pl.ds(k0, n)
        return jnp.exp2(jnp.maximum(freq[2, ks] * rows[2][x][:n] - freq[3, ks], 0.0))

    def put(j, x, k0, n, value):
        out[rows_of(j, x, k0, n), :] = value

    def lat_prepare(lat_forward, group):
        pltpu.make_async_copy(lat_in.at[group], lat_in.at[group], lat_recv.at[group]).wait()
        j = group * SPAN
        sign = 1.0 if lat_forward else -1.0
        speeds = [sign * dirs[4 * (j + i) + 1] for i in range(SPAN)]
        speed = jnp.where(lane < EDGE, speeds[2], jnp.where(lane < 2 * EDGE, speeds[1], speeds[0]))
        for k0, n in BLOCKS:
            ks = pl.ds(k0, n)
            spot = spot_all[:n]
            from_south = lat_in[group, 0, ks] * has_south
            from_north = lat_in[group, 1, ks] * has_north
            _, p1, p2, pd = coefficients(freq[0, ks], speed[:n])
            value = jnp.where(spot < 2, from_south, from_north) - packed[group, ks]
            one = 1 if lat_forward else LANES - 1
            near, next_spot, down_spot = (2, 3, 1) if lat_forward else (1, 0, 2)
            up_one = pltpu.roll(value, one, 1)
            up_two = pltpu.roll(value, (2 * one) % LANES, 1)
            down = pltpu.roll(value, LANES - one, 1)
            value = p2 * jnp.where((spot == near) | (spot == next_spot), up_two, 0.0)
            value = value + p1 * jnp.where(spot == near, up_one, 0.0)
            value = value - pd * jnp.where(spot == down_spot, down, 0.0)
            merged[ks] = pltpu.roll(value, LANES - EDGE * (SPAN - 1), 1)

    def lat_cells(lat_forward, group, jl):
        j = group * SPAN + jl
        jp = jnp.maximum(j - 2, 0)
        rows = rows_at(jp)
        two, one = (2, LANES - 1) if lat_forward else (LANES - 2, 1)
        for k0, n in BLOCKS:
            ks = pl.ds(k0, n)
            p0, p1, p2, pd = (coef[j, 4 + i, ks] for i in range(4))
            window = merged[ks]
            merged[ks] = pltpu.roll(window, EDGE, 1)
            for x in range(CELLS):
                f = along_lon[j, x, ks]
                extra = jnp.where(edge[:n], pltpu.roll(window, LANES - 2 - SIDE * x, 1), 0.0)
                shifted = pltpu.roll(f, two, 1)
                odd = pltpu.roll(p1 * shifted - pd * f, one, 1)
                value = (odd + extra) + (p0 * f + p2 * shifted)
                value = value * sea_b[x, :n]
                here, ahead = f_prev[1, x, ks], f_prev[0, x, ks]
                flux, moved = refract(rows, x, k0, n, here, ahead, g_prev[x, ks])
                put(jp, x, k0, n, moved * growth(rows, x, k0, n))
                g_prev[x, ks] = flux
                f_prev[1, x, ks] = ahead
                f_prev[0, x, ks] = value
                e_sum[x, ks] += value

    def lat_group(lat_forward, group):
        lat_prepare(lat_forward, group)

        def body(jl, carry):
            lat_cells(lat_forward, group, jl)
            if lat_forward:

                @pl.when(group * SPAN + jl < 2)
                def _():
                    field[group * SPAN + jl] = f_prev[0]

            return carry

        lax.fori_loop(0, SPAN, body, 0)

    def finish_wind():
        pltpu.make_async_copy(wrecv.at[pl.ds(0, 31)], wrecv.at[pl.ds(0, 31)], w_recv).wait()
        table = jnp.concatenate([wrecv[i] for i in range(32)], axis=0)
        halves = []
        for part in range(2):
            spot = lane32 + part * LANES
            source = spot // CAP
            q = spot - source * CAP
            mine = source == row
            for comp in range(2):
                got = jnp.where(mine, take(table, q + comp * CAP), 0.0)
                halves.append(jnp.sum(got, axis=0, keepdims=True))
        slot = slots[...]
        low_slot = jnp.minimum(slot, LANES - 1)
        high_slot = jnp.maximum(slot - LANES, 0)
        winds = []
        for comp in range(2):
            low_b = jnp.broadcast_to(halves[comp], (16, LANES))
            high_b = jnp.broadcast_to(halves[2 + comp], (16, LANES))
            got = jnp.where(slot < LANES, take(low_b, low_slot), take(high_b, high_slot))
            got = got * weights[...]
            half = got[0:8] + got[8:16]
            winds.append(half[0:4] + half[4:8])
        wind_out[0] = winds[0]
        wind_out[1] = winds[1]
        for x in range(CELLS):
            u_b[x] = jnp.broadcast_to(winds[0][x : x + 1], (8, LANES))
            v_b[x] = jnp.broadcast_to(winds[1][x : x + 1], (8, LANES))

    lax.fori_loop(FIRST, DEPTH, send_group, 0)

    def prepare(j, carry):
        for k0, n in BLOCKS:
            ks = pl.ds(k0, n)
            for axis in range(2):
                speed = jnp.abs(jnp.full((n, LANES), dirs[4 * j + axis], jnp.float32))
                for i, value in enumerate(coefficients(freq[0, ks], speed)):
                    coef[j, 4 * axis + i, ks] = value
        return carry

    lax.fori_loop(0, DIRS, prepare, 0)
    whole.wait()

    def run(g, carry):
        turn = (g >= GROUPS) & (g < 3 * GROUPS)

        @pl.when(g < 4 * GROUPS - DEPTH)
        def _():
            send_group(g + DEPTH, 0)

        @pl.when((g < 4 * GROUPS) & jnp.logical_not(turn))
        def _():
            lon_group(True, g)

        @pl.when(turn)
        def _():
            lon_group(False, g)

        @pl.when(g == LAG)
        def _():
            finish_wind()

        @pl.when((g >= LAG) & (g < LAG + 2 * GROUPS))
        def _():
            lat_group(True, g - LAG)

        @pl.when(g >= LAG + 2 * GROUPS)
        def _():
            lat_group(False, g - LAG)

        return carry

    lax.fori_loop(0, 4 * GROUPS + LAG, run, 0)

    def close(x, carry):
        def row_of(jp):
            d = [dirs[4 * jp + i] for i in range(4)]
            return r0_b[x] * d[2] - r1_b[x] * d[3], u_b[x] * d[0] + v_b[x] * d[1]

        rows = [row_of(jp) for jp in CLOSING]
        for k0, n in BLOCKS:
            ks = pl.ds(k0, n)
            f0 = field[0, x, ks]
            line = (f_prev[1, x, ks], f_prev[0, x, ks], f0, field[1, x, ks])
            flux = g_prev[x, ks]
            for i, jp in enumerate(CLOSING):
                rate, along = (part[:n] for part in rows[i])
                now = (freq[1, ks] * rate) * jnp.where(rate > 0.0, line[i], line[i + 1])
                moved = (line[i] - now) + flux
                grow = jnp.exp2(jnp.maximum(freq[2, ks] * along - freq[3, ks], 0.0))
                put(jp, x, k0, n, moved * grow)
                flux = now
        energy = jnp.sum(e_sum[x], axis=0, keepdims=True) * (1.0 / (FREQ * DIRS))
        energy_out[pl.ds(x, 1)] = energy
        energy_out[pl.ds(x + 4, 1)] = energy
        return carry

    lax.fori_loop(0, CELLS, close, 0)

    pltpu.make_async_copy(halo, halo, lon_send).wait()
    for side in range(2):
        pltpu.make_async_copy(packed, packed, lat_send.at[side]).wait()
    pltpu.make_async_copy(wsend.at[pl.ds(0, 31)], wsend.at[pl.ds(0, 31)], w_send).wait()


CHUNK = 4


def finish_kernel(moved, energy, wind, decay, out, wind_out, stage, wstage, sem, wsem):
    wstage[...] = wind[...]
    wcopy = pltpu.make_async_copy(wstage, wind_out, wsem)
    wcopy.start()
    e = energy[...]
    square = e * e

    def copy(c):
        ks = pl.ds(c * CHUNK, CHUNK)
        return pltpu.make_async_copy(stage.at[ks], out.at[ks], sem.at[c])

    def chunk(c, carry):
        for i in range(CHUNK):
            k = c * CHUNK + i
            factor = jnp.exp2(-(decay[k] * square))
            stage[k] = moved[k] * factor[None]
        copy(c).start()
        return carry

    lax.fori_loop(0, FREQ // CHUNK, chunk, 0)
    for c in range(FREQ // CHUNK):
        copy(c).wait()
    wcopy.wait()


def local(
    lon_size,
    lat_size,
    spectrum,
    sea_mask,
    refraction,
    atm_wind,
    hour_fraction,
    send_cells,
    recv_slots,
    recv_weights,
):
    per_freq, per_dir, decay = tables()
    f32 = jnp.float32
    hbm = pl.BlockSpec(memory_space=pltpu.HBM)
    vmem = pl.BlockSpec(memory_space=pltpu.VMEM)
    smem = pl.BlockSpec(memory_space=pltpu.SMEM)
    moved, energy, wind = pl.pallas_call(
        functools.partial(exchange_kernel, lon_size, lat_size),
        name="exchange",
        out_shape=(
            pltpu.VMEM((FREQ * DIRS * CELLS, LANES), f32),
            pltpu.VMEM((8, LANES), f32),
            pltpu.VMEM((2, CELLS, LANES), f32),
        ),
        in_specs=[hbm] * 5 + [smem] + [hbm] * 4 + [smem],
        out_specs=(vmem, vmem, vmem),
        scratch_shapes=[
            pltpu.VMEM((FREQ * DIRS * CELLS, LANES), f32),
            pltpu.VMEM((DIRS, CELLS, FREQ, LANES), f32),
            pltpu.VMEM((2, CELLS, FREQ, LANES), f32),
            pltpu.VMEM((2, CELLS, FREQ, LANES), f32),
            pltpu.VMEM((DIRS, 8, FREQ, LANES), f32),
            pltpu.VMEM((4 * GROUPS, 3 * SPAN, FREQ, LANES), f32),
            pltpu.VMEM((4 * GROUPS, FREQ, LANES), f32),
            pltpu.VMEM((4 * GROUPS, 2, FREQ, LANES), f32),
            pltpu.VMEM((FREQ, LANES), f32),
            pltpu.VMEM((CELLS, FREQ, LANES), f32),
            pltpu.VMEM((CELLS, FREQ, LANES), f32),
            pltpu.VMEM((CELLS, LANES), jnp.int32),
            pltpu.VMEM((2, CELLS, LANES), f32),
            pltpu.VMEM((2, 2, LANES), f32),
            pltpu.VMEM((1, 192), jnp.int32),
            pltpu.VMEM((16, LANES), jnp.int32),
            pltpu.VMEM((16, LANES), f32),
            pltpu.VMEM((4, FREQ, LANES), f32),
            pltpu.VMEM((CELLS, 8, LANES), f32),
            pltpu.VMEM((CELLS, 8, LANES), f32),
            pltpu.VMEM((CELLS, 8, LANES), f32),
            pltpu.VMEM((CELLS, 8, LANES), f32),
            pltpu.VMEM((CELLS, 8, LANES), f32),
            pltpu.VMEM((32, 1, LANES), f32),
            pltpu.VMEM((32, 1, LANES), f32),
            pltpu.SemaphoreType.DMA((7,)),
            pltpu.SemaphoreType.DMA,
            pltpu.SemaphoreType.DMA,
            pltpu.SemaphoreType.DMA((4 * GROUPS,)),
            pltpu.SemaphoreType.DMA((2,)),
            pltpu.SemaphoreType.DMA((4 * GROUPS,)),
            pltpu.SemaphoreType.DMA,
            pltpu.SemaphoreType.DMA,
        ],
        compiler_params=pltpu.CompilerParams(
            collective_id=0, has_side_effects=True, vmem_limit_bytes=54 << 20
        ),
    )(
        spectrum.reshape(FREQ, DIRS, CELLS, 1, LANES),
        spectrum.reshape(FREQ * DIRS * CELLS, LANES),
        sea_mask,
        refraction,
        atm_wind,
        hour_fraction,
        send_cells,
        recv_slots.reshape(4 * CELLS, LANES),
        recv_weights.reshape(4 * CELLS, LANES),
        jnp.asarray(per_freq),
        jnp.asarray(per_dir),
    )
    result, wind = pl.pallas_call(
        finish_kernel,
        name="finish",
        out_shape=(
            jax.ShapeDtypeStruct((FREQ, DIRS // 2, 8, LANES), f32),
            jax.ShapeDtypeStruct((2, CELLS, LANES), f32),
        ),
        in_specs=[vmem, vmem, vmem, smem],
        out_specs=(hbm, hbm),
        scratch_shapes=[
            pltpu.VMEM((FREQ, DIRS // 2, 8, LANES), f32),
            pltpu.VMEM((2, CELLS, LANES), f32),
            pltpu.SemaphoreType.DMA((FREQ // CHUNK,)),
            pltpu.SemaphoreType.DMA,
        ],
        compiler_params=pltpu.CompilerParams(vmem_limit_bytes=40 << 20),
    )(moved.reshape(FREQ, DIRS // 2, 8, LANES), energy, wind, jnp.asarray(decay))
    return result.reshape(FREQ, DIRS, CELLS, LANES), wind


def solution(mesh):
    in_specs = (
        P(None, None, "lon", "lat"),
        P("lon", "lat"),
        P(None, "lon", "lat"),
        P(None, None, ("lon", "lat")),
        P(),
        P(("lon", "lat"), None),
        P(None, "lon", "lat"),
        P(None, "lon", "lat"),
    )
    out_specs = (P(None, None, "lon", "lat"), P(None, "lon", "lat"))
    body = functools.partial(local, mesh.shape["lon"], mesh.shape["lat"])
    return jax.shard_map(body, mesh=mesh, in_specs=in_specs, out_specs=out_specs, check_vma=False)
```

```python
import functools
import math

import jax
import jax.numpy as jnp
import numpy as np
from jax import lax
from jax.experimental import pallas as pl
from jax.experimental.pallas import tpu as pltpu
from jax.sharding import PartitionSpec as P

FREQ = 36
DIRS = 36
QUAD = 9
SPAN = 3
GROUPS = 3
SIDE = 4
EDGE = SIDE * 4
LANES = 128
CELLS = 4
CAP = 6
BLOCKS = ((0, 8), (8, 8), (16, 8), (24, 8), (32, 4))
FIRST = 2
DEPTH = 9
CLOSING = (DIRS - 2, DIRS - 1, 0)
LAG = 5
LOG2E = math.log2(math.e)
MESH = pl.DeviceIdType.MESH


def tables():
    k = np.arange(FREQ, dtype=np.float64)
    freq = 0.035 * 1.1**k
    ratio = 0.035 / freq
    rel = freq / freq[-1]
    slow = 2.0 * math.pi * freq / 9.81
    rows = np.stack(
        [0.9 * ratio, np.sqrt(ratio), LOG2E * 0.05 * rel * slow, LOG2E * 0.05 * rel]
    )
    per_freq = np.broadcast_to(rows[:, :, None], (4, FREQ, LANES)).astype(np.float32)
    decay = (LOG2E * 0.8 * rel * 4.0).astype(np.float32)
    theta = (np.arange(DIRS) + 0.5) * 2.0 * math.pi / DIRS
    phi = (np.arange(DIRS) + 1.0) * 2.0 * math.pi / DIRS
    per_dir = np.stack([np.cos(theta), np.sin(theta), np.sin(phi), np.cos(phi)], axis=1)
    return per_freq, per_dir.reshape(-1).astype(np.float32), decay


def coefficients(rate, speed):
    a = rate * speed
    third = a * a * (1.0 / 6.0)
    g = a * (third - 1.0 / 6.0)
    b = a * ((third + 1.0 / 3.0) - 0.5 * a)
    p1 = (a - b) - (g + g)
    p0 = (1.0 - p1) - (g - b)
    return p0, p1, g, b


def take(table, index):
    return jnp.take_along_axis(table, index, axis=1, mode="promise_in_bounds")


def exchange_kernel(
    lon_size,
    lat_size,
    spec,
    spec_rows,
    sea_hbm,
    refr_hbm,
    atm_hbm,
    hour,
    cells_hbm,
    slots_hbm,
    weights_hbm,
    freq_hbm,
    dirs,
    out,
    energy_out,
    wind_out,
    nat,
    along_lon,
    field,
    f_prev,
    coef,
    halo,
    packed,
    lat_in,
    merged,
    g_prev,
    e_sum,
    sea_i,
    refr,
    atm,
    cells,
    slots,
    weights,
    freq,
    sea_b,
    r0_b,
    r1_b,
    u_b,
    v_b,
    wsend,
    wrecv,
    in_sem,
    x_sem,
    lon_send,
    lon_recv,
    lat_send,
    lat_recv,
    w_send,
    w_recv,
):
    me = lax.axis_index("lon")
    la = lax.axis_index("lat")
    right = lax.rem(me + 1, lon_size)
    left = lax.rem(me + lon_size - 1, lon_size)
    north = lax.rem(la + 1, lat_size)
    south = lax.rem(la + lat_size - 1, lat_size)

    barrier = pltpu.get_barrier_semaphore()

    small = [
        (atm_hbm, atm),
        (cells_hbm, cells),
        (sea_hbm, sea_i),
        (refr_hbm, refr),
        (slots_hbm, slots),
        (weights_hbm, weights),
        (freq_hbm, freq),
    ]
    small = [
        pltpu.make_async_copy(src, dst, in_sem.at[i]) for i, (src, dst) in enumerate(small)
    ]
    for copy in small:
        copy.start()

    def greet(d, carry):
        pl.semaphore_signal(
            barrier, inc=1, device_id=(lax.rem(me + d, lon_size), la), device_id_type=MESH
        )
        return carry

    lax.fori_loop(1, lon_size, greet, 0)
    for peer in (north, south):
        pl.semaphore_signal(barrier, inc=1, device_id=(me, peer), device_id_type=MESH)

    whole = pltpu.make_async_copy(spec_rows, nat, x_sem)
    whole.start()
    pl.semaphore_wait(barrier, lon_size + 1)

    def send_lon(j, x, slot, peer):
        pltpu.make_async_remote_copy(
            src_ref=spec.at[:, j, x, 0, :],
            dst_ref=halo.at[j // SPAN, (j % SPAN) * 3 + slot],
            send_sem=lon_send,
            recv_sem=lon_recv.at[j // SPAN],
            device_id=(peer, la),
            device_id_type=MESH,
        ).start()

    def send_group(group, carry):
        turned = (group >= GROUPS) & (group < 3 * GROUPS)
        cell = jnp.where(turned, 1, 2)
        peer = jnp.where(turned, left, right)

        def one(jl, inner):
            j = group * SPAN + jl
            send_lon(j, 3, 0, right)
            send_lon(j, 0, 1, left)
            send_lon(j, cell, 2, peer)
            return inner

        lax.fori_loop(0, SPAN, one, 0)
        return carry

    lax.fori_loop(0, FIRST, send_group, 0)

    for copy in small:
        copy.wait()

    late = hour[0]
    wind = (1.0 - late) * atm[0] + late * atm[1]
    row = lax.broadcasted_iota(jnp.int32, (32, LANES), 0)
    lane32 = lax.broadcasted_iota(jnp.int32, (32, LANES), 1)
    six = lane32 - (lane32 // CAP) * CAP
    place = row * CAP + six
    tail = jnp.concatenate([cells[:, LANES:], jnp.zeros((1, 64), jnp.int32)], axis=1)
    head_b = jnp.broadcast_to(cells[:, :LANES], (32, LANES))
    tail_b = jnp.broadcast_to(tail, (32, LANES))
    low = take(head_b, jnp.minimum(place, LANES - 1))
    high = take(tail_b, jnp.maximum(place - LANES, 0))
    index = jnp.where(place < LANES, low, high)
    u_pick = take(jnp.broadcast_to(wind[0:1], (32, LANES)), index)
    v_pick = take(jnp.broadcast_to(wind[1:2], (32, LANES)), index)
    pick = jnp.where(lane32 < CAP, u_pick, v_pick)
    for i in range(32):
        wsend[i] = pick[i : i + 1]

    def send_wind(d, carry):
        peer = lax.rem(me + d, lon_size)
        pltpu.make_async_remote_copy(
            src_ref=wsend.at[peer],
            dst_ref=wrecv.at[me],
            send_sem=w_send,
            recv_sem=w_recv,
            device_id=(peer, la),
            device_id_type=MESH,
        ).start()
        return carry

    lax.fori_loop(1, lon_size, send_wind, 0)
    wrecv[me] = wsend[me]

    sea = sea_i[...].astype(jnp.float32)
    r0 = refr[0]
    r1 = refr[1]
    for x in range(CELLS):
        sea_b[x] = jnp.broadcast_to(sea[x : x + 1], (8, LANES))
        r0_b[x] = jnp.broadcast_to(r0[x : x + 1], (8, LANES))
        r1_b[x] = jnp.broadcast_to(r1[x : x + 1], (8, LANES))
    e_sum[...] = jnp.zeros_like(e_sum)

    lane = lax.broadcasted_iota(jnp.int32, (8, LANES), 1)
    spot_all = lane & (SIDE - 1)
    edge = (lane >= LANES - 2) | (lane < 2)

    def rows_of(j, x, k0, n):
        return pl.ds(k0 * (DIRS * CELLS) + j * CELLS + x, n, stride=DIRS * CELLS)

    def lon_wait(group):
        pltpu.make_async_copy(halo.at[group], halo.at[group], lon_recv.at[group]).wait()

    def lon_cells(lon_forward, group, jl):
        j = group * SPAN + jl
        for k0, n in BLOCKS:
            ks = pl.ds(k0, n)
            p0, p1, p2, pd = (coef[j, i, ks] for i in range(4))
            before = halo[group, 3 * jl, ks]
            after = halo[group, 3 * jl + 1, ks]
            far = halo[group, 3 * jl + 2, ks]
            own = [nat[rows_of(j, x, k0, n), :] for x in range(CELLS)]
            if lon_forward:
                line = [far, before] + own + [after]
            else:
                line = [far, after] + own[::-1] + [before]
            pack = pltpu.roll(packed[group, ks], EDGE, 1)
            for i in range(CELLS):
                x = i if lon_forward else CELLS - 1 - i
                value = (p0 * line[i + 2] + p1 * line[i + 1]) + (
                    p2 * line[i] - pd * line[i + 3]
                )
                value = value * sea_b[x, :n]
                along_lon[j, x, ks] = value
                start = SIDE * x
                inside = (lane[:n] >= start) & (lane[:n] < start + SIDE)
                pack = jnp.where(inside, pltpu.roll(value, start + 2, 1), pack)
            packed[group, ks] = pack

    def lon_group(lon_forward, group):
        lon_wait(group)

        def body(jl, carry):
            lon_cells(lon_forward, group, jl)
            return carry

        lax.fori_loop(0, SPAN, body, 0)
        lat_send_edges(group)

    def lat_send_edges(group):
        for side, peer in enumerate((north, south)):
            pltpu.make_async_remote_copy(
                src_ref=packed.at[group],
                dst_ref=lat_in.at[group, side],
                send_sem=lat_send.at[side],
                recv_sem=lat_recv.at[group],
                device_id=(me, peer),
                device_id_type=MESH,
            ).start()

    has_south = (la > 0).astype(jnp.float32)
    has_north = (la < lat_size - 1).astype(jnp.float32)

    def rows_at(jp):
        d = [dirs[4 * jp + i] for i in range(4)]
        rates = [r0_b[x] * d[2] - r1_b[x] * d[3] for x in range(CELLS)]
        signs = [rate > 0.0 for rate in rates]
        along = [u_b[x] * d[0] + v_b[x] * d[1] for x in range(CELLS)]
        return rates, signs, along

    def refract(rows, x, k0, n, here, ahead, behind):
        rates, signs, _ = rows
        flux = (freq[1, pl.ds(k0, n)] * rates[x][:n]) * jnp.where(signs[x][:n], here, ahead)
        return flux, (here - flux) + behind

    def growth(rows, x, k0, n):
        ks = pl.ds(k0, n)
        return jnp.exp2(jnp.maximum(freq[2, ks] * rows[2][x][:n] - freq[3, ks], 0.0))

    def put(j, x, k0, n, value):
        out[rows_of(j, x, k0, n), :] = value

    def lat_prepare(lat_forward, group):
        pltpu.make_async_copy(lat_in.at[group], lat_in.at[group], lat_recv.at[group]).wait()
        j = group * SPAN
        sign = 1.0 if lat_forward else -1.0
        speeds = [sign * dirs[4 * (j + i) + 1] for i in range(SPAN)]
        speed = jnp.where(lane < EDGE, speeds[2], jnp.where(lane < 2 * EDGE, speeds[1], speeds[0]))
        for k0, n in BLOCKS:
            ks = pl.ds(k0, n)
            spot = spot_all[:n]
            from_south = lat_in[group, 0, ks] * has_south
            from_north = lat_in[group, 1, ks] * has_north
            _, p1, p2, pd = coefficients(freq[0, ks], speed[:n])
            value = jnp.where(spot < 2, from_south, from_north) - packed[group, ks]
            one = 1 if lat_forward else LANES - 1
            near, next_spot, down_spot = (2, 3, 1) if lat_forward else (1, 0, 2)
            up_one = pltpu.roll(value, one, 1)
            up_two = pltpu.roll(value, (2 * one) % LANES, 1)
            down = pltpu.roll(value, LANES - one, 1)
            value = p2 * jnp.where((spot == near) | (spot == next_spot), up_two, 0.0)
            value = value + p1 * jnp.where(spot == near, up_one, 0.0)
            value = value - pd * jnp.where(spot == down_spot, down, 0.0)
            merged[ks] = pltpu.roll(value, LANES - EDGE * (SPAN - 1), 1)

    def lat_cells(lat_forward, group, jl):
        j = group * SPAN + jl
        jp = jnp.maximum(j - 2, 0)
        rows = rows_at(jp)
        two, one = (2, LANES - 1) if lat_forward else (LANES - 2, 1)
        for k0, n in BLOCKS:
            ks = pl.ds(k0, n)
            p0, p1, p2, pd = (coef[j, 4 + i, ks] for i in range(4))
            window = merged[ks]
            merged[ks] = pltpu.roll(window, EDGE, 1)
            for x in range(CELLS):
                f = along_lon[j, x, ks]
                extra = jnp.where(edge[:n], pltpu.roll(window, LANES - 2 - SIDE * x, 1), 0.0)
                shifted = pltpu.roll(f, two, 1)
                odd = pltpu.roll(p1 * shifted - pd * f, one, 1)
                value = (odd + extra) + (p0 * f + p2 * shifted)
                value = value * sea_b[x, :n]
                here, ahead = f_prev[1, x, ks], f_prev[0, x, ks]
                flux, moved = refract(rows, x, k0, n, here, ahead, g_prev[x, ks])
                put(jp, x, k0, n, moved * growth(rows, x, k0, n))
                g_prev[x, ks] = flux
                f_prev[1, x, ks] = ahead
                f_prev[0, x, ks] = value
                e_sum[x, ks] += value

    def lat_group(lat_forward, group):
        lat_prepare(lat_forward, group)

        def body(jl, carry):
            lat_cells(lat_forward, group, jl)
            if lat_forward:

                @pl.when(group * SPAN + jl < 2)
                def _():
                    field[group * SPAN + jl] = f_prev[0]

            return carry

        lax.fori_loop(0, SPAN, body, 0)

    def finish_wind():
        pltpu.make_async_copy(wrecv.at[pl.ds(0, 31)], wrecv.at[pl.ds(0, 31)], w_recv).wait()
        table = jnp.concatenate([wrecv[i] for i in range(32)], axis=0)
        halves = []
        for part in range(2):
            spot = lane32 + part * LANES
            source = spot // CAP
            q = spot - source * CAP
            mine = source == row
            for comp in range(2):
                got = jnp.where(mine, take(table, q + comp * CAP), 0.0)
                halves.append(jnp.sum(got, axis=0, keepdims=True))
        slot = slots[...]
        low_slot = jnp.minimum(slot, LANES - 1)
        high_slot = jnp.maximum(slot - LANES, 0)
        winds = []
        for comp in range(2):
            low_b = jnp.broadcast_to(halves[comp], (16, LANES))
            high_b = jnp.broadcast_to(halves[2 + comp], (16, LANES))
            got = jnp.where(slot < LANES, take(low_b, low_slot), take(high_b, high_slot))
            got = got * weights[...]
            half = got[0:8] + got[8:16]
            winds.append(half[0:4] + half[4:8])
        wind_out[0] = winds[0]
        wind_out[1] = winds[1]
        for x in range(CELLS):
            u_b[x] = jnp.broadcast_to(winds[0][x : x + 1], (8, LANES))
            v_b[x] = jnp.broadcast_to(winds[1][x : x + 1], (8, LANES))

    lax.fori_loop(FIRST, DEPTH, send_group, 0)

    def prepare(j, carry):
        for k0, n in BLOCKS:
            ks = pl.ds(k0, n)
            for axis in range(2):
                speed = jnp.abs(jnp.full((n, LANES), dirs[4 * j + axis], jnp.float32))
                for i, value in enumerate(coefficients(freq[0, ks], speed)):
                    coef[j, 4 * axis + i, ks] = value
        return carry

    lax.fori_loop(0, DIRS, prepare, 0)
    whole.wait()

    def run(g, carry):
        turn = (g >= GROUPS) & (g < 3 * GROUPS)

        @pl.when(g < 4 * GROUPS - DEPTH)
        def _():
            send_group(g + DEPTH, 0)

        @pl.when((g < 4 * GROUPS) & jnp.logical_not(turn))
        def _():
            lon_group(True, g)

        @pl.when(turn)
        def _():
            lon_group(False, g)

        @pl.when(g == LAG)
        def _():
            finish_wind()

        @pl.when((g >= LAG) & (g < LAG + 2 * GROUPS))
        def _():
            lat_group(True, g - LAG)

        @pl.when(g >= LAG + 2 * GROUPS)
        def _():
            lat_group(False, g - LAG)

        return carry

    lax.fori_loop(0, 4 * GROUPS + LAG, run, 0)

    def close(x, carry):
        def row_of(jp):
            d = [dirs[4 * jp + i] for i in range(4)]
            return r0_b[x] * d[2] - r1_b[x] * d[3], u_b[x] * d[0] + v_b[x] * d[1]

        rows = [row_of(jp) for jp in CLOSING]
        for k0, n in BLOCKS:
            ks = pl.ds(k0, n)
            f0 = field[0, x, ks]
            line = (f_prev[1, x, ks], f_prev[0, x, ks], f0, field[1, x, ks])
            flux = g_prev[x, ks]
            for i, jp in enumerate(CLOSING):
                rate, along = (part[:n] for part in rows[i])
                now = (freq[1, ks] * rate) * jnp.where(rate > 0.0, line[i], line[i + 1])
                moved = (line[i] - now) + flux
                grow = jnp.exp2(jnp.maximum(freq[2, ks] * along - freq[3, ks], 0.0))
                put(jp, x, k0, n, moved * grow)
                flux = now
        energy = jnp.sum(e_sum[x], axis=0, keepdims=True) * (1.0 / (FREQ * DIRS))
        energy_out[pl.ds(x, 1)] = energy
        energy_out[pl.ds(x + 4, 1)] = energy
        return carry

    lax.fori_loop(0, CELLS, close, 0)

    pltpu.make_async_copy(halo, halo, lon_send).wait()
    for side in range(2):
        pltpu.make_async_copy(packed, packed, lat_send.at[side]).wait()
    pltpu.make_async_copy(wsend.at[pl.ds(0, 31)], wsend.at[pl.ds(0, 31)], w_send).wait()


CHUNK = 4


def finish_kernel(moved, energy, wind, decay, out, wind_out, stage, wstage, sem, wsem):
    wstage[...] = wind[...]
    wcopy = pltpu.make_async_copy(wstage, wind_out, wsem)
    wcopy.start()
    e = energy[...]
    square = e * e

    def copy(c):
        ks = pl.ds(c * CHUNK, CHUNK)
        return pltpu.make_async_copy(stage.at[ks], out.at[ks], sem.at[c])

    def chunk(c, carry):
        for i in range(CHUNK):
            k = c * CHUNK + i
            factor = jnp.exp2(-(decay[k] * square))
            stage[k] = moved[k] * factor[None]
        copy(c).start()
        return carry

    lax.fori_loop(0, FREQ // CHUNK, chunk, 0)
    for c in range(FREQ // CHUNK):
        copy(c).wait()
    wcopy.wait()


def local(
    lon_size,
    lat_size,
    spectrum,
    sea_mask,
    refraction,
    atm_wind,
    hour_fraction,
    send_cells,
    recv_slots,
    recv_weights,
):
    per_freq, per_dir, decay = tables()
    f32 = jnp.float32
    hbm = pl.BlockSpec(memory_space=pltpu.HBM)
    vmem = pl.BlockSpec(memory_space=pltpu.VMEM)
    smem = pl.BlockSpec(memory_space=pltpu.SMEM)
    moved, energy, wind = pl.pallas_call(
        functools.partial(exchange_kernel, lon_size, lat_size),
        name="exchange",
        out_shape=(
            pltpu.VMEM((FREQ * DIRS * CELLS, LANES), f32),
            pltpu.VMEM((8, LANES), f32),
            pltpu.VMEM((2, CELLS, LANES), f32),
        ),
        in_specs=[hbm] * 5 + [smem] + [hbm] * 4 + [smem],
        out_specs=(vmem, vmem, vmem),
        scratch_shapes=[
            pltpu.VMEM((FREQ * DIRS * CELLS, LANES), f32),
            pltpu.VMEM((DIRS, CELLS, FREQ, LANES), f32),
            pltpu.VMEM((2, CELLS, FREQ, LANES), f32),
            pltpu.VMEM((2, CELLS, FREQ, LANES), f32),
            pltpu.VMEM((DIRS, 8, FREQ, LANES), f32),
            pltpu.VMEM((4 * GROUPS, 3 * SPAN, FREQ, LANES), f32),
            pltpu.VMEM((4 * GROUPS, FREQ, LANES), f32),
            pltpu.VMEM((4 * GROUPS, 2, FREQ, LANES), f32),
            pltpu.VMEM((FREQ, LANES), f32),
            pltpu.VMEM((CELLS, FREQ, LANES), f32),
            pltpu.VMEM((CELLS, FREQ, LANES), f32),
            pltpu.VMEM((CELLS, LANES), jnp.int32),
            pltpu.VMEM((2, CELLS, LANES), f32),
            pltpu.VMEM((2, 2, LANES), f32),
            pltpu.VMEM((1, 192), jnp.int32),
            pltpu.VMEM((16, LANES), jnp.int32),
            pltpu.VMEM((16, LANES), f32),
            pltpu.VMEM((4, FREQ, LANES), f32),
            pltpu.VMEM((CELLS, 8, LANES), f32),
            pltpu.VMEM((CELLS, 8, LANES), f32),
            pltpu.VMEM((CELLS, 8, LANES), f32),
            pltpu.VMEM((CELLS, 8, LANES), f32),
            pltpu.VMEM((CELLS, 8, LANES), f32),
            pltpu.VMEM((32, 1, LANES), f32),
            pltpu.VMEM((32, 1, LANES), f32),
            pltpu.SemaphoreType.DMA((7,)),
            pltpu.SemaphoreType.DMA,
            pltpu.SemaphoreType.DMA,
            pltpu.SemaphoreType.DMA((4 * GROUPS,)),
            pltpu.SemaphoreType.DMA((2,)),
            pltpu.SemaphoreType.DMA((4 * GROUPS,)),
            pltpu.SemaphoreType.DMA,
            pltpu.SemaphoreType.DMA,
        ],
        compiler_params=pltpu.CompilerParams(
            collective_id=0, has_side_effects=True, vmem_limit_bytes=54 << 20
        ),
    )(
        spectrum.reshape(FREQ, DIRS, CELLS, 1, LANES),
        spectrum.reshape(FREQ * DIRS * CELLS, LANES),
        sea_mask,
        refraction,
        atm_wind,
        hour_fraction,
        send_cells,
        recv_slots.reshape(4 * CELLS, LANES),
        recv_weights.reshape(4 * CELLS, LANES),
        jnp.asarray(per_freq),
        jnp.asarray(per_dir),
    )
    result, wind = pl.pallas_call(
        finish_kernel,
        name="finish",
        out_shape=(
            jax.ShapeDtypeStruct((FREQ, DIRS // 2, 8, LANES), f32),
            jax.ShapeDtypeStruct((2, CELLS, LANES), f32),
        ),
        in_specs=[vmem, vmem, vmem, smem],
        out_specs=(hbm, hbm),
        scratch_shapes=[
            pltpu.VMEM((FREQ, DIRS // 2, 8, LANES), f32),
            pltpu.VMEM((2, CELLS, LANES), f32),
            pltpu.SemaphoreType.DMA((FREQ // CHUNK,)),
            pltpu.SemaphoreType.DMA,
        ],
        compiler_params=pltpu.CompilerParams(vmem_limit_bytes=40 << 20),
    )(moved.reshape(FREQ, DIRS // 2, 8, LANES), energy, wind, jnp.asarray(decay))
    return result.reshape(FREQ, DIRS, CELLS, LANES), wind


def solution(mesh):
    in_specs = (
        P(None, None, "lon", "lat"),
        P("lon", "lat"),
        P(None, "lon", "lat"),
        P(None, None, ("lon", "lat")),
        P(),
        P(("lon", "lat"), None),
        P(None, "lon", "lat"),
        P(None, "lon", "lat"),
    )
    out_specs = (P(None, None, "lon", "lat"), P(None, "lon", "lat"))
    body = functools.partial(local, mesh.shape["lon"], mesh.shape["lat"])
    return jax.shard_map(body, mesh=mesh, in_specs=in_specs, out_specs=out_specs, check_vma=False)
```
